128 devices in a mesh: freq: 4 (over z_hi, core), vis: 32 (over z_lo, y, x).
Axes of the slice: x: 4, y: 4, z: 4 (z_hi: 2, z_lo: 2; z = z_hi * 2 + z_lo), core: 2. Of those that a mesh axis runs over, the one named last changes fastest.
Arguments:
- model_input: bfloat16 [2, 16, 512, 512], P(None, 'freq', 'vis'), parts along dimension 1, may hold values from -6 to 6
- w_kernels: bfloat16 [64, 2, 128, 128], P('freq'), parts along dimension 0, may hold values from -0.375 to 0.375
- visibilities: bfloat16 [4096, 2, 128, 128], P(('freq', 'vis')), parts along dimension 0, may hold values from -6 to 6
- tile_facet: int32 [4096], P(('freq', 'vis')), parts along dimension 0, may hold values from 0 to 3
- tile_patch: int32 [4096], P(('freq', 'vis')), parts along dimension 0, may hold values from 0 to 15
- tile_wplane: int32 [4096], P(('freq', 'vis')), parts along dimension 0, may hold values from 0 to 15
- tile_count: int32 [128], P(('freq', 'vis')), parts along dimension 0, may hold values from 16 to 32, as said below
Outputs:
- residual_image: float32 [16, 512, 512], P('freq', 'vis'), parts along dimension 0
The draws below stay inside these ranges and needn't reach their ends.
There are 4 independent parts, one for each index of `freq`. The reference program is written for one: setup_inputs(seed, part) draws one part's arguments, and reference() takes and returns one part's arrays. A program takes and returns all parts, laid end to end along the dimension named above; each array names one. Nothing has to cross between parts.
Inputs may be any that keep to these rules, and one draw needn't show every extreme that they name: `tile_count`: each device's live tiles fill its first slots; some device holds exactly 32.
All inputs are finite; a program needn't handle non-finite values.
Results may differ from the reference program's by a relative error of at most 0.02.
Values may be sent and summed in bfloat16 or wider, within the bound.
A program may use at most 128 MiB of HBM per device.

```python
import math
import jax
import jax.numpy as jnp
from jax import lax

P_SIZE = 512
S = 128
F = 4
WPLANES = 16
CYCLES = 2
TILE_CAP = 32
NP = 16
TILES = 1024


def draw_tile_count(key, part):
    devices = TILES // TILE_CAP
    draw_one, draw_two = jax.random.split(key)
    counts = jax.random.randint(draw_one, (devices,), TILE_CAP // 2, TILE_CAP + 1)
    busiest = jax.random.randint(draw_two, (), 0, devices)
    return jnp.where(jnp.arange(devices) == busiest, TILE_CAP, counts).astype(jnp.int32)


def place_ends(array, rng, smallest, largest):
    longest = array.shape.index(max(array.shape))
    spots = []
    for shift in (0, 1):
        where = [jax.random.randint(jax.random.fold_in(rng, axis), (), 0, length) for axis, length in enumerate(array.shape)]
        where[longest] = (where[longest] + shift) % array.shape[longest]
        spots.append(tuple(where))
    return array.at[spots[0]].set(smallest).at[spots[1]].set(largest)


def level_of(own_key, shape, pieces, low, high):
    def one(axis_at, parts):
        heights = jax.random.uniform(jax.random.fold_in(jax.random.fold_in(own_key, 6), axis_at), (parts,), jnp.float32, low / len(pieces), high / len(pieces))
        return jnp.repeat(jnp.exp(heights), shape[axis_at] // parts).reshape((-1,) + (1,) * (len(shape) - axis_at - 1))

    loudness = one(*pieces[0])
    for cut in pieces[1:]:
        loudness = loudness * one(*cut)
    return loudness


def centred(own_key, extent, scale, bound, pieces=(), kind=jnp.bfloat16):
    level = level_of(own_key, extent, pieces, -0.22, 0.18) if pieces else 1.0
    result = jax.random.normal(own_key, extent, jnp.float32) * scale * level
    return jnp.minimum(jnp.maximum(result, -bound), bound).astype(kind)


def setup_inputs(seed: int = 0, part: int = 0) -> dict:
    keys = jax.random.split(jax.random.key(seed), 8)
    part_splits = jax.random.split(jax.random.fold_in(keys[7], part), 8)
    model_input = centred(part_splits[0], (CYCLES, F, P_SIZE, P_SIZE), 1.0, 6.0, ((2, 32),))
    w_kernels = centred(part_splits[1], (WPLANES, 2, S, S), (2 * S) ** -0.5, 0.375)
    visibilities = centred(part_splits[2], (TILES, 2, S, S), 1.0, 6.0, ((0, 32),))
    tile_facet = place_ends(jax.random.randint(part_splits[3], (TILES,), 0, F), jax.random.fold_in(part_splits[3], 1), 0, F - 1).astype(jnp.int32)
    tile_patch = place_ends(jax.random.randint(part_splits[4], (TILES,), 0, NP), jax.random.fold_in(part_splits[4], 1), 0, NP - 1).astype(jnp.int32)
    tile_wplane = place_ends(jax.random.randint(part_splits[5], (TILES,), 0, WPLANES), jax.random.fold_in(part_splits[5], 1), 0, WPLANES - 1).astype(jnp.int32)
    tile_count = draw_tile_count(jax.random.fold_in(jax.random.fold_in(keys[7], part), 71), part)
    return dict(model_input=model_input, w_kernels=w_kernels, visibilities=visibilities, tile_facet=tile_facet, tile_patch=tile_patch, tile_wplane=tile_wplane, tile_count=tile_count)


loop_gain = 0.5

def dft_tables(first_row, row_count, length):
    row_ids = first_row + jnp.arange(row_count, dtype=jnp.int32)
    col_ids = jnp.arange(length, dtype=jnp.int32)
    phases = row_ids[:, None] * col_ids[None, :] % length
    angles = phases.astype(jnp.float32) * (2.0 * math.pi / length)
    scaling = 1.0 / math.sqrt(length)
    return (jnp.cos(angles) * scaling, jnp.sin(angles) * scaling)

def product(pattern, first_op, second_op):
    return jnp.einsum(pattern, first_op, second_op, precision=lax.Precision.HIGHEST)

def to_half(value):
    return lax.optimization_barrier(value.astype(jnp.bfloat16)).astype(jnp.float32)

def tile_terms(patches, kernel, observed, alive):
    patch_real, patch_imag = (patches[:, 0], patches[:, 1])
    kern_real, kern_imag = (kernel[:, 0], kernel[:, 1])
    mid_real = to_half(product('tij,tjk->tik', kern_real, patch_real) - product('tij,tjk->tik', kern_imag, patch_imag))
    mid_imag = to_half(product('tij,tjk->tik', kern_real, patch_imag) + product('tij,tjk->tik', kern_imag, patch_real))
    model_real = product('tij,tkj->tik', mid_real, kern_real) - product('tij,tkj->tik', mid_imag, kern_imag)
    model_imag = product('tij,tkj->tik', mid_real, kern_imag) + product('tij,tkj->tik', mid_imag, kern_real)
    resid_real = to_half((observed[:, 0] - model_real) * alive[:, None, None])
    resid_imag = to_half((observed[:, 1] - model_imag) * alive[:, None, None])
    back_real = to_half(product('tji,tjk->tik', kern_real, resid_real) + product('tji,tjk->tik', kern_imag, resid_imag))
    back_imag = to_half(product('tji,tjk->tik', kern_real, resid_imag) - product('tji,tjk->tik', kern_imag, resid_real))
    out_real = product('tij,tjk->tik', back_real, kern_real) + product('tij,tjk->tik', back_imag, kern_imag)
    out_imag = product('tij,tjk->tik', back_imag, kern_real) - product('tij,tjk->tik', back_real, kern_imag)
    return jnp.stack([out_real, out_imag], axis=1)

def reference(model_input, w_kernels, visibilities, tile_facet, tile_patch, tile_wplane, tile_count):
    devices = TILES // TILE_CAP
    cosine, sine = dft_tables(0, P_SIZE, P_SIZE)
    cosine_half = cosine.astype(jnp.bfloat16).astype(jnp.float32)
    sine_half = sine.astype(jnp.bfloat16).astype(jnp.float32)
    slots = (tile_facet * NP + tile_patch).astype(jnp.int32)
    alive = (jnp.arange(TILE_CAP, dtype=jnp.int32)[None, :] < tile_count[:, None]).astype(jnp.float32).reshape(TILES)
    weight = math.sqrt(F * NP / TILES)
    kernels = w_kernels.astype(jnp.float32)
    residual_image = jnp.zeros((F, P_SIZE, P_SIZE), jnp.float32)
    for cycle_index in range(CYCLES):
        if cycle_index == 0:
            sky_model = model_input[0].astype(jnp.float32)
        else:
            sky_model = to_half(model_input[cycle_index].astype(jnp.float32) + loop_gain * residual_image)
        half_real = to_half(product('fij,jk->fik', sky_model, cosine_half))
        half_imag = to_half(-product('fij,jk->fik', sky_model, sine_half))
        grid_real = to_half(product('ij,fjk->fik', cosine_half, half_real) + product('ij,fjk->fik', sine_half, half_imag))
        grid_imag = to_half(product('ij,fjk->fik', cosine_half, half_imag) - product('ij,fjk->fik', sine_half, half_real))
        full_grid = jnp.stack([grid_real, grid_imag], axis=1)
        patch_table = full_grid.reshape(F, 2, P_SIZE // S, S, P_SIZE // S, S).transpose(0, 2, 4, 1, 3, 5).reshape(F * NP, 2, S, S)

        def accumulate(running, tile_block):
            slot_ids, plane_ids, observed, live_block = tile_block
            tile_sums = tile_terms(patch_table[slot_ids], kernels[plane_ids], observed.astype(jnp.float32), live_block)
            return (running.at[slot_ids].add(tile_sums), None)
        blocks = (slots.reshape(devices, TILE_CAP), tile_wplane.reshape(devices, TILE_CAP), visibilities.reshape(devices, TILE_CAP, 2, S, S), alive.reshape(devices, TILE_CAP))
        summed, unused = lax.scan(accumulate, jnp.zeros((F * NP, 2, S, S), jnp.float32), blocks)
        resid_grid = summed.reshape(F, P_SIZE // S, P_SIZE // S, 2, S, S).transpose(0, 3, 1, 4, 2, 5).reshape(F, 2, P_SIZE, P_SIZE)
        spec_real = product('ij,fjk->fik', cosine, resid_grid[:, 0]) - product('ij,fjk->fik', sine, resid_grid[:, 1])
        spec_imag = product('ij,fjk->fik', cosine, resid_grid[:, 1]) + product('ij,fjk->fik', sine, resid_grid[:, 0])
        residual_image = (product('fij,jk->fik', spec_real, cosine) - product('fij,jk->fik', spec_imag, sine)) * weight
    return residual_image
```

```python
import functools
import math

import jax
import jax.numpy as jnp
import numpy as np
from jax import lax
from jax.experimental import pallas as pl
from jax.experimental.pallas import tpu as pltpu
from jax.sharding import PartitionSpec as P

P_SIZE = 512
S = 128
F = 4
WPLANES = 16
TILE_CAP = 32
NP = 16
SLOTS = F * NP
DEVICES = 32
ROWS = P_SIZE // DEVICES
TILES = TILE_CAP * DEVICES
WEIGHT = math.sqrt(F * NP / TILES)
LOOP_GAIN = 0.5
MESH = pl.DeviceIdType.MESH
BF16 = jnp.bfloat16
F32 = jnp.float32
VIS_CHUNK = 4


def dot(a, b):
    return lax.dot_general(a, b, (((1,), (0,)), ((), ())), preferred_element_type=F32)


def lanes(*parts):
    return jnp.concatenate(parts, axis=1)


def stack(*parts):
    return jnp.concatenate(parts, axis=0)


def regrid_kernel(
    facet_ref, patch_ref, plane_ref, count_ref, w_ref, vis_hbm, grid_ref, cnt_ref,
    vis_buf, back_op, term_op, acc, cnt_acc, sems,
):
    copies = [
        pltpu.make_async_copy(
            vis_hbm.at[pl.ds(k * VIS_CHUNK, VIS_CHUNK)],
            vis_buf.at[pl.ds(k * VIS_CHUNK, VIS_CHUNK)],
            sems.at[k],
        )
        for k in range(TILE_CAP // VIS_CHUNK)
    ]
    for copy in copies:
        copy.start()

    @pl.loop(0, WPLANES)
    def _(w):
        real, imag = w_ref[w, 0], w_ref[w, 1]
        back_op[w] = lanes(real.T, imag.T)
        term_op[w] = stack(lanes(real, -imag), lanes(imag, real))

    @pl.loop(0, SLOTS + 1)
    def _(s):
        acc[s] = jnp.zeros((S, 2 * S), F32)
        cnt_acc[s] = jnp.zeros((WPLANES, S), F32)

    for k, copy in enumerate(copies):
        copy.wait()
        for t in range(k * VIS_CHUNK, (k + 1) * VIS_CHUNK):
            patch, plane = patch_ref[t], plane_ref[t]
            slot = facet_ref[t] * NP + lax.rem(patch, 4) * 4 + lax.div(patch, 4)
            slot = jnp.where(t < count_ref[0], slot, SLOTS)
            real, imag = vis_buf[t, 0], vis_buf[t, 1]
            half = dot(lanes(real, imag), term_op[plane])
            half_real, half_imag = half[:, :S].astype(BF16), half[:, S:].astype(BF16)
            term = dot(
                back_op[plane], stack(lanes(half_real, half_imag), lanes(half_imag, -half_real))
            )
            acc[slot] += term
            cnt_acc[slot, pl.ds(plane, 1), :] += jnp.ones((1, S), F32)

    @pl.loop(0, SLOTS)
    def _(s):
        grid_ref[s] = acc[s].astype(BF16)
        cnt_ref[s] = cnt_acc[s].astype(BF16)


def regrid(w_kernels, visibilities, tile_facet, tile_patch, tile_wplane, tile_count):
    smem = pl.BlockSpec(memory_space=pltpu.SMEM)
    vmem = pl.BlockSpec(memory_space=pltpu.VMEM)
    return pl.pallas_call(
        regrid_kernel,
        out_shape=(
            jax.ShapeDtypeStruct((SLOTS, S, 2 * S), BF16),
            jax.ShapeDtypeStruct((SLOTS, WPLANES, S), BF16),
        ),
        in_specs=[smem] * 4 + [vmem, pl.BlockSpec(memory_space=pl.ANY)],
        out_specs=(vmem, vmem),
        scratch_shapes=[
            pltpu.VMEM((TILE_CAP, 2, S, S), BF16),
            pltpu.VMEM((WPLANES, S, 2 * S), BF16),
            pltpu.VMEM((WPLANES, 2 * S, 2 * S), BF16),
            pltpu.VMEM((SLOTS + 1, S, 2 * S), F32),
            pltpu.VMEM((SLOTS + 1, WPLANES, S), F32),
            pltpu.SemaphoreType.DMA((TILE_CAP // VIS_CHUNK,)),
        ],
        compiler_params=pltpu.CompilerParams(vmem_limit_bytes=40 << 20),
        name="regrid",
    )(tile_facet, tile_patch, tile_wplane, tile_count, w_kernels, visibilities)


def cycle_kernel(
    sky_ref, cs_ref, w_ref, cnt_ref, grid_hbm, out_ref,
    grid_buf, to_rows, to_cols, half_buf, column_buf, dirty_buf, dirty_in, u_buf, row_in,
    cnt_in, left_op, right_op, b_buf, wide_buf, grid_sems, send_sems, recv_sems, dirty_send, dirty_recv,
):
    me = lax.axis_index("vis")
    half_index = lax.rem(me, 2)
    column = lax.rem(lax.div(me, 2), 4)
    facet = lax.div(me, 8)

    grid_copies = [
        pltpu.make_async_copy(
            grid_hbm.at[pl.ds(f * NP, NP)], grid_buf.at[pl.ds(f * NP, NP)], grid_sems.at[f]
        )
        for f in range(F)
    ]
    for copy in grid_copies:
        copy.start()

    barrier = pltpu.get_barrier_semaphore()

    @pl.loop(1, DEVICES)
    def _(k):
        other = lax.rem(me + k, DEVICES)
        pl.semaphore_signal(barrier, inc=1, device_id={"vis": other}, device_id_type=MESH)

    for c in range(4):
        at, low = c * 2 * S, c * S
        to_cols[:, at:at + S] = cs_ref[0, :, low:low + S]
        to_cols[:, at + S:at + 2 * S] = -cs_ref[1, :, low:low + S]
        to_rows[at:at + S, :] = cs_ref[0, low:low + S, :]
        to_rows[at + S:at + 2 * S, :] = -cs_ref[1, low:low + S, :]

    def remote(src, dst, send, recv, other):
        return pltpu.make_async_remote_copy(
            src_ref=src, dst_ref=dst, send_sem=send, recv_sem=recv,
            device_id={"vis": other}, device_id_type=MESH,
        )

    def wait_for(ref, sem):
        pltpu.make_async_copy(ref, ref, sem).wait()

    def exchange_columns(stage):
        def piece(other):
            f, c = lax.div(other, 8), lax.rem(lax.div(other, 2), 4)
            return half_buf.at[
                stage,
                pl.ds(pl.multiple_of(f * ROWS, ROWS), ROWS),
                pl.ds(pl.multiple_of(c * 2 * S, 2 * S), 2 * S),
            ]

        def place():
            return column_buf.at[stage, me]

        @pl.loop(1, DEVICES)
        def _(k):
            other = lax.rem(me + k, DEVICES)
            remote(piece(other), place(), send_sems.at[2 * stage], recv_sems.at[2 * stage], other).start()

        pltpu.make_async_copy(piece(me), place(), recv_sems.at[2 * stage]).start()

    def exchange_rows(stage):
        def piece(other):
            return u_buf.at[stage, pl.ds(pl.multiple_of(other * ROWS, ROWS), ROWS), :]

        def place():
            block = column * 2 + half_index
            return row_in.at[stage, block, pl.ds(pl.multiple_of(facet * ROWS, ROWS), ROWS), :]

        @pl.loop(1, DEVICES)
        def _(k):
            other = lax.rem(me + k, DEVICES)
            remote(
                piece(other), place(), send_sems.at[2 * stage + 1], recv_sems.at[2 * stage + 1], other
            ).start()

        pltpu.make_async_copy(piece(me), place(), recv_sems.at[2 * stage + 1]).start()

    half_buf[0] = dot(sky_ref[0], to_cols[...]).astype(BF16)
    pl.semaphore_wait(barrier, DEVICES - 1)

    @pl.loop(1, DEVICES)
    def _(k):
        other = lax.rem(me + k, DEVICES)
        remote(cnt_ref.at[other], cnt_in.at[me], send_sems.at[4], recv_sems.at[4], other).start()

    pltpu.make_async_copy(cnt_ref.at[me], cnt_in.at[me], recv_sems.at[4]).start()
    exchange_columns(0)

    for f in range(F):
        grid_copies[f].wait()
        for c in range(4):
            at = f * NP + c * 4
            block = grid_buf[at:at + 4].reshape(P_SIZE, 2 * S)
            cosine_part, sine_part = dot(cs_ref[0], block), dot(cs_ref[1], block)
            wide_buf[:, c * 2 * S:c * 2 * S + S] = (cosine_part[:, :S] - sine_part[:, S:]).astype(BF16)
            wide_buf[:, c * 2 * S + S:(c + 1) * 2 * S] = (cosine_part[:, S:] + sine_part[:, :S]).astype(BF16)
        dirty_buf[f] = dot(wide_buf[...], to_rows[...]).astype(BF16)

        @pl.loop(1, DEVICES)
        def _(k):
            other = lax.rem(me + k, DEVICES)
            remote(
                dirty_buf.at[f, pl.ds(pl.multiple_of(other * ROWS, ROWS), ROWS), :],
                dirty_in.at[f, me], dirty_send.at[f], dirty_recv.at[f], other,
            ).start()

        pltpu.make_async_copy(
            dirty_buf.at[f, pl.ds(pl.multiple_of(me * ROWS, ROWS), ROWS), :],
            dirty_in.at[f, me], dirty_recv.at[f],
        ).start()

    @pl.loop(0, WPLANES)
    def _(w):
        real, imag = w_ref[w, 0], w_ref[w, 1]
        gram = dot(lanes(real.T, imag.T), stack(lanes(real, imag), lanes(imag, -real))).astype(BF16)
        gram_real, gram_imag = gram[:, :S], gram[:, S:]
        left_op[pl.ds(w * S, S), :] = gram
        right_op[pl.ds(w * 2 * S, S), :] = lanes(gram_real, -gram_imag)
        right_op[pl.ds(w * 2 * S + S, S), :] = lanes(gram_imag, gram_real)

    wait_for(cnt_in, recv_sems.at[4])
    counts = jnp.sum(cnt_in[...].astype(F32), axis=0)

    rows_at = pl.multiple_of(half_index * 2 * S, 2 * S)

    def model_rows(stage):
        wait_for(column_buf.at[stage], recv_sems.at[2 * stage])
        half = column_buf[stage].reshape(P_SIZE, 2 * S)
        turned = lanes(half[:, S:], -half[:, :S])
        grid = dot(cs_ref[0, pl.ds(rows_at, 2 * S), :], half) + dot(cs_ref[1, pl.ds(rows_at, 2 * S), :], turned)
        grid = grid.astype(BF16)
        for q in range(2):
            patch = grid[q * S:(q + 1) * S]
            operand = stack(patch, lanes(-patch[:, S:], patch[:, :S]))
            for w in range(WPLANES):
                part = dot(left_op[w * S:(w + 1) * S, :], operand)
                scale = counts[q, w:w + 1, :]
                b_buf[q * S:(q + 1) * S, w * 2 * S:(w + 1) * 2 * S] = (part * lanes(scale, scale)).astype(BF16)
        model = dot(b_buf[...], right_op[...]).astype(BF16)
        turned = lanes(-model[:, S:], model[:, :S])
        u_buf[stage] = (
            dot(cs_ref[0, :, pl.ds(rows_at, 2 * S)], model) + dot(cs_ref[1, :, pl.ds(rows_at, 2 * S)], turned)
        ).astype(BF16)
        exchange_rows(stage)
        wait_for(row_in.at[stage], recv_sems.at[2 * stage + 1])
        parts = [
            (row_in[stage, 2 * c].astype(F32) + row_in[stage, 2 * c + 1].astype(F32)).astype(BF16)
            for c in range(4)
        ]
        return dot(lanes(*parts), to_rows[...])

    image = model_rows(0)
    for f in range(F):
        wait_for(dirty_in.at[f], dirty_recv.at[f])
        dirty = jnp.sum(dirty_in[f].astype(F32), axis=0)
        out_ref[f * ROWS:(f + 1) * ROWS, :] = dirty
    residual = (out_ref[...] - image) * WEIGHT
    sky = (sky_ref[1].astype(F32) + LOOP_GAIN * residual).astype(BF16)
    half_buf[1] = dot(sky, to_cols[...]).astype(BF16)
    exchange_columns(1)
    image = model_rows(1)
    out_ref[...] = (out_ref[...] - image) * WEIGHT

    for stage in range(2):
        wait_for(column_buf.at[stage, pl.ds(0, DEVICES - 1)], send_sems.at[2 * stage])
        wait_for(u_buf.at[stage, pl.ds(0, P_SIZE - ROWS), :], send_sems.at[2 * stage + 1])
    wait_for(cnt_in.at[pl.ds(0, DEVICES - 1)], send_sems.at[4])
    for f in range(F):
        wait_for(dirty_in.at[f, pl.ds(0, DEVICES - 1)], dirty_send.at[f])


def cycles(sky, tables, w_kernels, counts, grid):
    vmem = pl.BlockSpec(memory_space=pltpu.VMEM)
    return pl.pallas_call(
        cycle_kernel,
        out_shape=jax.ShapeDtypeStruct((F * ROWS, P_SIZE), F32),
        in_specs=[vmem] * 4 + [pl.BlockSpec(memory_space=pl.ANY)],
        out_specs=vmem,
        scratch_shapes=[
            pltpu.VMEM((SLOTS, S, 2 * S), BF16),
            pltpu.VMEM((2 * P_SIZE, P_SIZE), BF16),
            pltpu.VMEM((P_SIZE, 2 * P_SIZE), BF16),
            pltpu.VMEM((2, F * ROWS, 2 * P_SIZE), BF16),
            pltpu.VMEM((2, DEVICES, ROWS, 2 * S), BF16),
            pltpu.VMEM((F, P_SIZE, P_SIZE), BF16),
            pltpu.VMEM((F, DEVICES, ROWS, P_SIZE), BF16),
            pltpu.VMEM((2, P_SIZE, 2 * S), BF16),
            pltpu.VMEM((2, 8, F * ROWS, 2 * S), BF16),
            pltpu.VMEM((DEVICES, 2, WPLANES, S), BF16),
            pltpu.VMEM((WPLANES * S, 2 * S), BF16),
            pltpu.VMEM((WPLANES * 2 * S, 2 * S), BF16),
            pltpu.VMEM((2 * S, WPLANES * 2 * S), BF16),
            pltpu.VMEM((P_SIZE, 2 * P_SIZE), BF16),
            pltpu.SemaphoreType.DMA((F,)),
            pltpu.SemaphoreType.DMA((5,)),
            pltpu.SemaphoreType.DMA((5,)),
            pltpu.SemaphoreType.DMA((F,)),
            pltpu.SemaphoreType.DMA((F,)),
        ],
        compiler_params=pltpu.CompilerParams(
            collective_id=0, has_side_effects=True, vmem_limit_bytes=48 << 20
        ),
        name="cycles",
    )(sky, tables, w_kernels, counts, grid)


def dft_tables():
    phases = np.outer(np.arange(P_SIZE), np.arange(P_SIZE)) % P_SIZE
    angles = phases * (2.0 * math.pi / P_SIZE)
    return (np.stack([np.cos(angles), np.sin(angles)]) / math.sqrt(P_SIZE)).astype(BF16)


def local(model_input, w_kernels, visibilities, tile_facet, tile_patch, tile_wplane, tile_count):
    grid, counts = regrid(w_kernels, visibilities, tile_facet, tile_patch, tile_wplane, tile_count)
    sky = model_input.reshape(2, F * ROWS, P_SIZE)
    counts = counts.reshape(DEVICES, 2, WPLANES, S)
    image = cycles(sky, jnp.asarray(dft_tables()), w_kernels, counts, grid)
    return image.reshape(F, ROWS, P_SIZE)


def solution(mesh):
    return jax.shard_map(
        local,
        mesh=mesh,
        in_specs=(
            P(None, "freq", "vis", None),
            P("freq", None, None, None),
            P(("freq", "vis"), None, None, None),
            P(("freq", "vis")),
            P(("freq", "vis")),
            P(("freq", "vis")),
            P(("freq", "vis")),
        ),
        out_specs=P("freq", "vis", None),
        check_vma=False,
    )
```

```python
import math

import jax
import jax.numpy as jnp
import numpy as np
from jax import lax
from jax.experimental import pallas as pl
from jax.experimental.pallas import tpu as pltpu
from jax.sharding import PartitionSpec as P

P_SIZE = 512
S = 128
F = 4
WPLANES = 16
TILE_CAP = 32
NP = 16
SLOTS = F * NP
DEVICES = 32
ROWS = P_SIZE // DEVICES
TILES = TILE_CAP * DEVICES
WEIGHT = math.sqrt(F * NP / TILES)
LOOP_GAIN = 0.5
MESH = pl.DeviceIdType.MESH
BF16 = jnp.bfloat16
F32 = jnp.float32
VIS_CHUNK = 4
CHUNKS = TILE_CAP // VIS_CHUNK


def dot(a, b):
    return lax.dot_general(a, b, (((1,), (0,)), ((), ())), preferred_element_type=F32)


def lanes(*parts):
    return jnp.concatenate(parts, axis=1)


def stack(*parts):
    return jnp.concatenate(parts, axis=0)


def imaging_kernel(
    facet_hbm, patch_hbm, plane_hbm, count_hbm, sky_hbm, cs_hbm, w_hbm, vis_hbm, out_ref,
    facet_ref, patch_ref, plane_ref, count_ref, sky_ref, cs_ref, w_ref, vis_buf,
    back_op, term_op, run_buf, grid_buf, to_rows, to_cols, half_buf, column_buf, u_buf, row_in,
    cnt_out, cnt_in, left_op, right_op, b_buf, wide_buf, model_buf,
    dirty_out, dirty_in, second_out, second_in, third_own, third_out, third_in,
    load_sems, vis_sems, send_sems, recv_sems, dirty_send, dirty_recv,
):
    me = lax.axis_index("vis")
    half_index = lax.rem(me, 2)
    column = lax.rem(lax.div(me, 2), 4)
    facet = lax.div(me, 8)
    at_x, at_y, at_z = lax.rem(me, 4), lax.rem(lax.div(me, 4), 4), lax.div(me, 16)

    loads = [
        pltpu.make_async_copy(src, dst, load_sems.at[k])
        for k, (src, dst) in enumerate(
            (
                (facet_hbm, facet_ref), (patch_hbm, patch_ref), (plane_hbm, plane_ref), (count_hbm, count_ref),
                (w_hbm, w_ref), (cs_hbm, cs_ref), (sky_hbm, sky_ref),
            )
        )
    ]
    vis_loads = [
        pltpu.make_async_copy(
            vis_hbm.at[pl.ds(k * VIS_CHUNK, VIS_CHUNK)],
            vis_buf.at[pl.ds(k * VIS_CHUNK, VIS_CHUNK)],
            vis_sems.at[k],
        )
        for k in range(CHUNKS)
    ]
    for copy in loads[:5] + vis_loads + loads[5:]:
        copy.start()

    barrier = pltpu.get_barrier_semaphore()

    @pl.loop(1, DEVICES)
    def _(k):
        other = lax.rem(me + k, DEVICES)
        pl.semaphore_signal(barrier, inc=1, device_id={"vis": other}, device_id_type=MESH)

    def remote(src, dst, send, recv, other):
        return pltpu.make_async_remote_copy(
            src_ref=src, dst_ref=dst, send_sem=send, recv_sem=recv,
            device_id={"vis": other}, device_id_type=MESH,
        )

    def wait_for(ref, sem):
        pltpu.make_async_copy(ref, ref, sem).wait()

    def to_all(piece, place, index):
        @pl.loop(1, DEVICES)
        def _(k):
            other = lax.rem(me + k, DEVICES)
            remote(piece(other), place, send_sems.at[index], recv_sems.at[index], other).start()

        pltpu.make_async_copy(piece(me), place, recv_sems.at[index]).start()

    def exchange_columns(stage):
        def piece(other):
            f, c = lax.div(other, 8), lax.rem(lax.div(other, 2), 4)
            return half_buf.at[
                stage,
                pl.ds(pl.multiple_of(f * ROWS, ROWS), ROWS),
                pl.ds(pl.multiple_of(c * 2 * S, 2 * S), 2 * S),
            ]

        to_all(piece, column_buf.at[stage, me], 2 * stage)

    def exchange_rows(stage):
        def piece(other):
            return u_buf.at[stage, pl.ds(pl.multiple_of(other * ROWS, ROWS), ROWS), :]

        place = row_in.at[
            stage, column * 2 + half_index, pl.ds(pl.multiple_of(facet * ROWS, ROWS), ROWS), :
        ]
        to_all(piece, place, 2 * stage + 1)

    for copy in loads[:4]:
        copy.wait()

    lane = lax.broadcasted_iota(jnp.int32, (1, S), 1)
    tile = lax.broadcasted_iota(jnp.int32, (TILE_CAP, S), 0)
    slot_row = jnp.full((1, S), SLOTS, jnp.int32)
    plane_row = jnp.full((1, S), WPLANES, jnp.int32)
    slot_column = jnp.full((TILE_CAP, S), SLOTS, jnp.int32)
    for t in range(TILE_CAP):
        patch = patch_ref[t]
        slot = facet_ref[t] * NP + lax.rem(patch, 4) * 4 + lax.div(patch, 4)
        slot = jnp.where(t < count_ref[0], slot, SLOTS)
        slot_row = jnp.where(lane == t, slot, slot_row)
        plane_row = jnp.where(lane == t, plane_ref[t], plane_row)
        slot_column = jnp.where(tile == t, slot, slot_column)
    tile_lane = lax.broadcasted_iota(jnp.int32, (TILE_CAP, S), 1)
    before = jnp.max(
        jnp.where((slot_column == slot_row) & (tile_lane < tile), tile_lane, -1), axis=1, keepdims=True
    )
    slot_lane = lax.broadcasted_iota(jnp.int32, (SLOTS, S), 1)
    member = lax.broadcasted_iota(jnp.int32, (SLOTS, S), 0) == slot_row
    last = jnp.max(jnp.where(member, slot_lane, -1), axis=1, keepdims=True)
    before = jnp.where(before < 0, TILE_CAP, before)
    last = jnp.where(last < 0, TILE_CAP, last)

    in_plane = jnp.where(
        lax.broadcasted_iota(jnp.int32, (WPLANES, S), 0) == plane_row, 1.0, 0.0
    )
    in_slot = jnp.where(member, 1.0, 0.0)
    pairs = stack(*[(in_plane * in_slot[s:s + 1, :]).astype(BF16) for s in range(SLOTS)])
    cnt_out[...] = dot(pairs, jnp.ones((S, S), BF16)).astype(BF16).reshape(DEVICES, 2, WPLANES, S)

    loads[4].wait()

    @pl.loop(0, WPLANES)
    def _(w):
        real, imag = w_ref[w, 0], w_ref[w, 1]
        back_op[w] = lanes(real.T, imag.T)
        term_op[w] = stack(lanes(real, -imag), lanes(imag, real))

    run_buf[TILE_CAP] = jnp.zeros((S, 2 * S), F32)
    for k in range(CHUNKS):
        vis_loads[k].wait()
        for t in range(k * VIS_CHUNK, (k + 1) * VIS_CHUNK):
            plane = plane_ref[t]
            real, imag = vis_buf[t, 0], vis_buf[t, 1]
            half = dot(lanes(real, imag), term_op[plane])
            half_real, half_imag = half[:, :S].astype(BF16), half[:, S:].astype(BF16)
            term = dot(
                back_op[plane], stack(lanes(half_real, half_imag), lanes(half_imag, -half_real))
            )
            run_buf[t] = term + run_buf[before[t, 0]]

    loads[5].wait()
    for c in range(4):
        at, low = c * 2 * S, c * S
        to_cols[:, at:at + S] = cs_ref[0, :, low:low + S]
        to_cols[:, at + S:at + 2 * S] = -cs_ref[1, :, low:low + S]
        to_rows[at:at + S, :] = cs_ref[0, low:low + S, :]
        to_rows[at + S:at + 2 * S, :] = -cs_ref[1, low:low + S, :]
    loads[6].wait()
    half_buf[0] = dot(sky_ref[0], to_cols[...]).astype(BF16)
    pl.semaphore_wait(barrier, DEVICES - 1)
    to_all(lambda other: cnt_out.at[other], cnt_in.at[me], 4)
    exchange_columns(0)

    def first_stage(f):
        for k in range(1, 4):
            if f % 2 == 0:
                x = lax.rem(at_x + k, 4)
                piece, other = dirty_out.at[f, :, :, x], at_z * 16 + at_y * 4 + x
            else:
                y = lax.rem(at_y + k, 4)
                piece, other = dirty_out.at[f, :, y], at_z * 16 + y * 4 + at_x
            remote(piece, dirty_in.at[f, k - 1], dirty_send.at[0, f], dirty_recv.at[0, f], other).start()

    def second_stage(f):
        wait_for(dirty_in.at[f], dirty_recv.at[0, f])
        mine = dirty_out[f, :, :, at_x] if f % 2 == 0 else dirty_out[f, :, at_y]
        total = mine.astype(F32)
        for k in range(3):
            total += dirty_in[f, k].astype(F32)
        second_out[f] = total.astype(BF16)
        for k in range(1, 4):
            if f % 2 == 0:
                step = lax.rem(at_y + k, 4)
                other = at_z * 16 + step * 4 + at_x
            else:
                step = lax.rem(at_x + k, 4)
                other = at_z * 16 + at_y * 4 + step
            remote(
                second_out.at[f, :, step], second_in.at[f, k - 1], dirty_send.at[1, f], dirty_recv.at[1, f], other
            ).start()

    def third_stage(f):
        wait_for(second_in.at[f], dirty_recv.at[1, f])
        total = second_out[f, :, at_y if f % 2 == 0 else at_x].astype(F32)
        for k in range(3):
            total += second_in[f, k].astype(F32)
        third_own[f] = total
        third_out[f] = total.astype(BF16)
        remote(
            third_out.at[f, 1 - at_z], third_in.at[f], dirty_send.at[2, f], dirty_recv.at[2, f],
            lax.rem(me + 16, DEVICES),
        ).start()

    def dirty_rows(f):
        wait_for(third_in.at[f], dirty_recv.at[2, f])
        return third_own[f, at_z] + third_in[f].astype(F32)

    for f in range(F):
        for s in range(NP):
            grid_buf[s] = run_buf[last[f * NP + s, 0]].astype(BF16)
        for c in range(4):
            block = grid_buf[c * 4:c * 4 + 4].reshape(P_SIZE, 2 * S)
            cosine_part, sine_part = dot(cs_ref[0], block), dot(cs_ref[1], block)
            wide_buf[:, c * 2 * S:c * 2 * S + S] = (cosine_part[:, :S] - sine_part[:, S:]).astype(BF16)
            wide_buf[:, c * 2 * S + S:(c + 1) * 2 * S] = (cosine_part[:, S:] + sine_part[:, :S]).astype(BF16)
        dirty_out[f] = dot(wide_buf[...], to_rows[...]).astype(BF16).reshape(2, 4, 4, ROWS, P_SIZE)
        first_stage(f)

    @pl.loop(0, WPLANES)
    def _(w):
        real, imag = w_ref[w, 0], w_ref[w, 1]
        gram = dot(back_op[w], stack(lanes(real, imag), lanes(imag, -real))).astype(BF16)
        gram_real, gram_imag = gram[:, :S], gram[:, S:]
        left_op[pl.ds(w * S, S), :] = gram
        right_op[pl.ds(w * 2 * S, S), :] = lanes(gram_real, -gram_imag)
        right_op[pl.ds(w * 2 * S + S, S), :] = lanes(gram_imag, gram_real)

    wait_for(cnt_in, recv_sems.at[4])
    counts = jnp.sum(cnt_in[...].astype(F32), axis=0)

    rows_at = pl.multiple_of(half_index * 2 * S, 2 * S)

    def model_slots(stage):
        wait_for(column_buf.at[stage], recv_sems.at[2 * stage])
        half = column_buf[stage].reshape(P_SIZE, 2 * S)
        turned = lanes(half[:, S:], -half[:, :S])
        grid = dot(cs_ref[0, pl.ds(rows_at, 2 * S), :], half) + dot(cs_ref[1, pl.ds(rows_at, 2 * S), :], turned)
        grid = grid.astype(BF16)
        for q in range(2):
            patch = grid[q * S:(q + 1) * S]
            operand = stack(patch, lanes(-patch[:, S:], patch[:, :S]))
            for w in range(WPLANES):
                part = dot(left_op[w * S:(w + 1) * S, :], operand)
                scale = counts[q, w:w + 1, :]
                b_buf[q * S:(q + 1) * S, w * 2 * S:(w + 1) * 2 * S] = (part * lanes(scale, scale)).astype(BF16)
        model = dot(b_buf[...], right_op[...]).astype(BF16)
        turned = lanes(-model[:, S:], model[:, :S])
        u_buf[stage] = (
            dot(cs_ref[0, :, pl.ds(rows_at, 2 * S)], model) + dot(cs_ref[1, :, pl.ds(rows_at, 2 * S)], turned)
        ).astype(BF16)
        exchange_rows(stage)

    def model_rows(stage):
        wait_for(row_in.at[stage], recv_sems.at[2 * stage + 1])
        parts = [
            (row_in[stage, 2 * c].astype(F32) + row_in[stage, 2 * c + 1].astype(F32)).astype(BF16)
            for c in range(4)
        ]
        return dot(lanes(*parts), to_rows[...])

    model_slots(0)
    second_stage(0)
    second_stage(1)
    model_buf[...] = model_rows(0)
    third_stage(0)
    third_stage(1)
    second_stage(2)
    second_stage(3)
    third_stage(2)
    third_stage(3)
    for f in range(F):
        out_ref[f * ROWS:(f + 1) * ROWS, :] = dirty_rows(f)
    residual = (out_ref[...] - model_buf[...]) * WEIGHT
    sky = (sky_ref[1].astype(F32) + LOOP_GAIN * residual).astype(BF16)
    half_buf[1] = dot(sky, to_cols[...]).astype(BF16)
    exchange_columns(1)
    model_slots(1)
    out_ref[...] = (out_ref[...] - model_rows(1)) * WEIGHT

    for stage in range(2):
        wait_for(column_buf.at[stage, pl.ds(0, DEVICES - 1)], send_sems.at[2 * stage])
        wait_for(u_buf.at[stage, pl.ds(0, P_SIZE - ROWS), :], send_sems.at[2 * stage + 1])
    wait_for(cnt_in.at[pl.ds(0, DEVICES - 1)], send_sems.at[4])
    for f in range(F):
        wait_for(dirty_in.at[f], dirty_send.at[0, f])
        wait_for(second_in.at[f], dirty_send.at[1, f])
        wait_for(third_in.at[f], dirty_send.at[2, f])


def imaging(*operands):
    hbm = pl.BlockSpec(memory_space=pltpu.HBM)
    return pl.pallas_call(
        imaging_kernel,
        out_shape=jax.ShapeDtypeStruct((F * ROWS, P_SIZE), F32),
        in_specs=[hbm] * 8,
        out_specs=pl.BlockSpec(memory_space=pltpu.VMEM),
        scratch_shapes=[
            pltpu.SMEM((TILE_CAP,), jnp.int32),
            pltpu.SMEM((TILE_CAP,), jnp.int32),
            pltpu.SMEM((TILE_CAP,), jnp.int32),
            pltpu.SMEM((1,), jnp.int32),
            pltpu.VMEM((2, F * ROWS, P_SIZE), BF16),
            pltpu.VMEM((2, P_SIZE, P_SIZE), BF16),
            pltpu.VMEM((WPLANES, 2, S, S), BF16),
            pltpu.VMEM((TILE_CAP, 2, S, S), BF16),
            pltpu.VMEM((WPLANES, S, 2 * S), BF16),
            pltpu.VMEM((WPLANES, 2 * S, 2 * S), BF16),
            pltpu.VMEM((TILE_CAP + 1, S, 2 * S), F32),
            pltpu.VMEM((NP, S, 2 * S), BF16),
            pltpu.VMEM((2 * P_SIZE, P_SIZE), BF16),
            pltpu.VMEM((P_SIZE, 2 * P_SIZE), BF16),
            pltpu.VMEM((2, F * ROWS, 2 * P_SIZE), BF16),
            pltpu.VMEM((2, DEVICES, ROWS, 2 * S), BF16),
            pltpu.VMEM((2, P_SIZE, 2 * S), BF16),
            pltpu.VMEM((2, 8, F * ROWS, 2 * S), BF16),
            pltpu.VMEM((DEVICES, 2, WPLANES, S), BF16),
            pltpu.VMEM((DEVICES, 2, WPLANES, S), BF16),
            pltpu.VMEM((WPLANES * S, 2 * S), BF16),
            pltpu.VMEM((WPLANES * 2 * S, 2 * S), BF16),
            pltpu.VMEM((2 * S, WPLANES * 2 * S), BF16),
            pltpu.VMEM((P_SIZE, 2 * P_SIZE), BF16),
            pltpu.VMEM((F * ROWS, P_SIZE), F32),
            pltpu.VMEM((F, 2, 4, 4, ROWS, P_SIZE), BF16),
            pltpu.VMEM((F, 3, 2, 4, ROWS, P_SIZE), BF16),
            pltpu.VMEM((F, 2, 4, ROWS, P_SIZE), BF16),
            pltpu.VMEM((F, 3, 2, ROWS, P_SIZE), BF16),
            pltpu.VMEM((F, 2, ROWS, P_SIZE), F32),
            pltpu.VMEM((F, 2, ROWS, P_SIZE), BF16),
            pltpu.VMEM((F, ROWS, P_SIZE), BF16),
            pltpu.SemaphoreType.DMA((7,)),
            pltpu.SemaphoreType.DMA((CHUNKS,)),
            pltpu.SemaphoreType.DMA((5,)),
            pltpu.SemaphoreType.DMA((5,)),
            pltpu.SemaphoreType.DMA((3, F)),
            pltpu.SemaphoreType.DMA((3, F)),
        ],
        compiler_params=pltpu.CompilerParams(
            collective_id=0, has_side_effects=True, vmem_limit_bytes=56 << 20
        ),
        name="imaging",
    )(*operands)


def dft_tables():
    phases = np.outer(np.arange(P_SIZE), np.arange(P_SIZE)) % P_SIZE
    angles = phases * (2.0 * math.pi / P_SIZE)
    return (np.stack([np.cos(angles), np.sin(angles)]) / math.sqrt(P_SIZE)).astype(BF16)


def local(model_input, w_kernels, visibilities, tile_facet, tile_patch, tile_wplane, tile_count):
    sky = model_input.reshape(2, F * ROWS, P_SIZE)
    image = imaging(
        tile_facet, tile_patch, tile_wplane, tile_count,
        sky, jnp.asarray(dft_tables()), w_kernels, visibilities,
    )
    return image.reshape(F, ROWS, P_SIZE)


def solution(mesh):
    return jax.shard_map(
        local,
        mesh=mesh,
        in_specs=(
            P(None, "freq", "vis", None),
            P("freq", None, None, None),
            P(("freq", "vis"), None, None, None),
            P(("freq", "vis")),
            P(("freq", "vis")),
            P(("freq", "vis")),
            P(("freq", "vis")),
        ),
        out_specs=P("freq", "vis", None),
        check_vma=False,
    )
```

```python
import math

import jax
import jax.numpy as jnp
import numpy as np
from jax import lax
from jax.experimental import pallas as pl
from jax.experimental.pallas import tpu as pltpu
from jax.sharding import PartitionSpec as P

P_SIZE = 512
S = 128
F = 4
WPLANES = 16
TILE_CAP = 32
NP = 16
SLOTS = F * NP
DEVICES = 32
ROWS = P_SIZE // DEVICES
TILES = TILE_CAP * DEVICES
WEIGHT = math.sqrt(F * NP / TILES)
LOOP_GAIN = 0.5
MESH = pl.DeviceIdType.MESH
BF16 = jnp.bfloat16
F32 = jnp.float32
VIS_CHUNK = 4
CHUNKS = TILE_CAP // VIS_CHUNK
EXT = S + ROWS
WIDE = 3 * S


def dot(a, b):
    return lax.dot_general(a, b, (((1,), (0,)), ((), ())), preferred_element_type=F32)


def lanes(*parts):
    return jnp.concatenate(parts, axis=1)


def stack(*parts):
    return jnp.concatenate(parts, axis=0)


def owner(device):
    z, y, x = lax.div(device, 16), lax.rem(lax.div(device, 4), 4), lax.rem(device, 4)
    a, b = y + z * (x - y), x + z * (y - x)
    return 2 * z + lax.div(a, 2), lax.rem(a, 2), b


def static_owner(device):
    z, y, x = device // 16, device // 4 % 4, device % 4
    a, b = (x, y) if z else (y, x)
    return 2 * z + a // 2, a % 2, b


def slot_of(f, row, column):
    return f * NP + column * 4 + row


def where_equal(shape, rule):
    row = lax.broadcasted_iota(jnp.int32, shape, 0)
    column = lax.broadcasted_iota(jnp.int32, shape, 1)
    return rule(row, column).astype(BF16)


def one_if(condition):
    return jnp.where(condition, 1.0, 0.0)


def imaging_kernel(
    facet_hbm, patch_hbm, plane_hbm, count_hbm, sky_hbm, cs_hbm, edge_hbm, w_hbm, vis_hbm, out_ref,
    facet_ref, patch_ref, plane_ref, count_ref, sky_ref, cs_ref, edge_ref, w_ref, vis_buf,
    back_op, term_op, run_buf, grid_buf, to_rows, to_cols, half_buf, column_buf, u_buf, row_in,
    cnt_out, cnt_in, left_op, right_op, b_buf, spread_buf,
    first_out, first_in, second_out, second_in, third_own, third_out, third_in,
    load_sems, vis_sems, send_sems, recv_sems, dirty_send, dirty_recv,
):
    me = lax.axis_index("vis")
    facet, row_block, column = owner(me)
    at_x, at_y, at_z = lax.rem(me, 4), lax.rem(lax.div(me, 4), 4), lax.div(me, 16)

    loads = [
        pltpu.make_async_copy(src, dst, load_sems.at[k])
        for k, (src, dst) in enumerate(
            (
                (facet_hbm, facet_ref), (patch_hbm, patch_ref), (plane_hbm, plane_ref), (count_hbm, count_ref),
                (w_hbm, w_ref), (cs_hbm, cs_ref), (sky_hbm, sky_ref), (edge_hbm, edge_ref),
            )
        )
    ]
    vis_loads = [
        pltpu.make_async_copy(
            vis_hbm.at[pl.ds(k * VIS_CHUNK, VIS_CHUNK)],
            vis_buf.at[pl.ds(k * VIS_CHUNK, VIS_CHUNK)],
            vis_sems.at[k],
        )
        for k in range(CHUNKS)
    ]
    for copy in loads[:5] + vis_loads + loads[5:]:
        copy.start()

    barrier = pltpu.get_barrier_semaphore()

    @pl.loop(1, DEVICES)
    def _(k):
        other = lax.rem(me + k, DEVICES)
        pl.semaphore_signal(barrier, inc=1, device_id={"vis": other}, device_id_type=MESH)

    def remote(src, dst, send, recv, other):
        return pltpu.make_async_remote_copy(
            src_ref=src, dst_ref=dst, send_sem=send, recv_sem=recv,
            device_id={"vis": other}, device_id_type=MESH,
        )

    def wait_for(ref, sem):
        pltpu.make_async_copy(ref, ref, sem).wait()

    def to_all(piece, place, index):
        @pl.loop(1, DEVICES)
        def _(k):
            other = lax.rem(me + k, DEVICES)
            remote(piece(other), place, send_sems.at[index], recv_sems.at[index], other).start()

        pltpu.make_async_copy(piece(me), place, recv_sems.at[index]).start()

    def exchange_columns(stage):
        def piece(other):
            f, _, c = owner(other)
            return half_buf.at[
                stage,
                pl.ds(pl.multiple_of(f * ROWS, ROWS), ROWS),
                pl.ds(pl.multiple_of(c * WIDE, WIDE), WIDE),
            ]

        to_all(piece, column_buf.at[stage, me], 2 * stage)

    def exchange_rows(stage):
        def piece(other):
            return u_buf.at[stage, pl.ds(pl.multiple_of(other * ROWS, ROWS), ROWS), :]

        place = row_in.at[
            stage, column * 2 + row_block, pl.ds(pl.multiple_of(facet * ROWS, ROWS), ROWS), :
        ]
        to_all(piece, place, 2 * stage + 1)

    for copy in loads[:4]:
        copy.wait()

    lane = lax.broadcasted_iota(jnp.int32, (1, S), 1)
    tile = lax.broadcasted_iota(jnp.int32, (TILE_CAP, S), 0)
    slot_row = jnp.full((1, S), SLOTS, jnp.int32)
    plane_row = jnp.full((1, S), WPLANES, jnp.int32)
    slot_column = jnp.full((TILE_CAP, S), SLOTS, jnp.int32)
    for t in range(TILE_CAP):
        patch = patch_ref[t]
        slot = facet_ref[t] * NP + lax.rem(patch, 4) * 4 + lax.div(patch, 4)
        slot = jnp.where(t < count_ref[0], slot, SLOTS)
        slot_row = jnp.where(lane == t, slot, slot_row)
        plane_row = jnp.where(lane == t, plane_ref[t], plane_row)
        slot_column = jnp.where(tile == t, slot, slot_column)
    tile_lane = lax.broadcasted_iota(jnp.int32, (TILE_CAP, S), 1)
    before = jnp.max(
        jnp.where((slot_column == slot_row) & (tile_lane < tile), tile_lane, -1), axis=1, keepdims=True
    )
    slot_lane = lax.broadcasted_iota(jnp.int32, (SLOTS, S), 1)
    member = lax.broadcasted_iota(jnp.int32, (SLOTS, S), 0) == slot_row
    last = jnp.max(jnp.where(member, slot_lane, -1), axis=1, keepdims=True)
    before = jnp.where(before < 0, TILE_CAP, before)
    last = jnp.where(last < 0, TILE_CAP, last)

    in_plane = jnp.where(
        lax.broadcasted_iota(jnp.int32, (WPLANES, S), 0) == plane_row, 1.0, 0.0
    )
    in_slot = jnp.where(member, 1.0, 0.0)
    held = []
    for device in range(DEVICES):
        f, r, c = static_owner(device)
        held += [slot_of(f, r, c), slot_of(f, 3 - r, 3 - c)]
    pairs = stack(*[(in_plane * in_slot[s:s + 1, :]).astype(BF16) for s in held])
    cnt_out[...] = dot(pairs, jnp.ones((S, S), BF16)).astype(BF16).reshape(DEVICES, 2, WPLANES, S)

    loads[4].wait()

    @pl.loop(0, WPLANES)
    def _(w):
        real, imag = w_ref[w, 0], w_ref[w, 1]
        back_op[w] = lanes(real.T, imag.T)
        term_op[w] = stack(lanes(real, -imag), lanes(imag, real))

    run_buf[TILE_CAP] = jnp.zeros((S, 2 * S), F32)
    for k in range(CHUNKS):
        vis_loads[k].wait()
        for t in range(k * VIS_CHUNK, (k + 1) * VIS_CHUNK):
            plane = plane_ref[t]
            real, imag = vis_buf[t, 0], vis_buf[t, 1]
            half = dot(lanes(real, imag), term_op[plane])
            half_real, half_imag = half[:, :S].astype(BF16), half[:, S:].astype(BF16)
            term = dot(
                back_op[plane], stack(lanes(half_real, half_imag), lanes(half_imag, -half_real))
            )
            run_buf[t] = term + run_buf[before[t, 0]]

    loads[5].wait()
    loads[7].wait()
    row = lax.broadcasted_iota(jnp.int32, (S, P_SIZE), 0)
    for c in range(4):
        at, low, edge = c * WIDE, c * S, (c + 1) % 4 * S
        to_cols[:, at:at + S] = cs_ref[0, :, low:low + S]
        to_cols[:, at + S:at + 2 * S] = -cs_ref[1, :, low:low + S]
        to_cols[:, at + 2 * S:at + WIDE] = edge_ref[:, low:low + S]
        to_rows[at:at + S, :] = cs_ref[0, low:low + S, :]
        to_rows[at + S:at + 2 * S, :] = -cs_ref[1, low:low + S, :]
        cosine_row = cs_ref[0, edge:edge + 1, :].astype(F32)
        sine_row = cs_ref[1, edge:edge + 1, :].astype(F32)
        to_rows[at + 2 * S:at + WIDE, :] = jnp.where(
            row == 0, cosine_row, jnp.where(row == 1, -sine_row, 0.0)
        ).astype(BF16)
    loads[6].wait()
    half_buf[0] = dot(sky_ref[0], to_cols[...]).astype(BF16)

    mirror_rows = where_equal(
        (S, 2 * S), lambda i, k: one_if(((k == S - i) & (i > 0)) | ((k == S) & (i == 0)))
    )
    mirror_cols = where_equal(
        (2 * S, S), lambda k, j: one_if(((k == S - j) & (j > 0)) | ((k == S) & (j == 0)))
    )
    far_cols = where_equal(
        (2 * S, S), lambda k, j: one_if(((k == S - j) & (j > 0)) | ((k == S + 1) & (j == 0)))
    )
    near_spread = where_equal(
        (S, 2 * S), lambda j, k: one_if(((k == S - j) & (j > 0)) | ((k == S) & (j == 0)))
    )
    far_spread = where_equal(
        (S, 2 * S), lambda j, k: one_if(((k == S - j) & (j > 0)) | ((k == S + 1) & (j == 0)))
    )
    unfold_rows = where_equal((S, EXT), lambda i, k: one_if(k == S - i))
    fold_rows = where_equal((EXT, S), lambda k, i: one_if(k == S - i))
    quarter_turn = where_equal(
        (S, S), lambda i, j: one_if((i == 0) & (j == 1)) - one_if((i == 1) & (j == 0))
    )
    pick_ends = where_equal(
        (ROWS, 2 * S), lambda i, k: one_if(((i == 0) & (k == 0)) | ((i == 1) & (k == S)))
    )
    put_real = where_equal((ROWS, S), lambda i, j: one_if((i == 1) & (j == 0)))
    put_imag = where_equal((ROWS, S), lambda i, j: one_if((i == 1) & (j == 1)))

    def contract(a, b, dims):
        return lax.dot_general(a, b, (dims, ((), ())), preferred_element_type=F32)

    @pl.loop(0, WPLANES)
    def _(w):
        real, imag = w_ref[w, 0], w_ref[w, 1]
        gram = dot(back_op[w], stack(lanes(real, imag), lanes(imag, -real))).astype(BF16)
        gram_real, gram_imag = gram[:, :S], gram[:, S:]
        left_op[pl.ds(w * S, S), :] = gram
        right_op[pl.ds(w * 2 * S, S), :] = lanes(gram_real, -gram_imag)
        right_op[pl.ds(w * 2 * S + S, S), :] = lanes(gram_imag, gram_real)

    pl.semaphore_wait(barrier, DEVICES - 1)
    to_all(lambda other: cnt_out.at[other], cnt_in.at[me], 4)
    exchange_columns(0)

    def first_stage(f):
        for k in range(1, 4):
            if f < 2:
                step = lax.rem(at_x + k, 4)
                other = at_z * 16 + at_y * 4 + step
            else:
                step = lax.rem(at_y + k, 4)
                other = at_z * 16 + step * 4 + at_x
            remote(
                first_out.at[f, :, step], first_in.at[f, k - 1], dirty_send.at[0, f], dirty_recv.at[0, f], other
            ).start()

    def second_stage(group):
        for f in (2 * group, 2 * group + 1):
            wait_for(first_in.at[f], dirty_recv.at[0, f])
            total = first_out[f, :, at_x if group == 0 else at_y].astype(F32)
            for k in range(3):
                total += first_in[f, k].astype(F32)
            second_out[group, 2 * (f % 2):2 * (f % 2) + 2] = total.astype(BF16)
        for k in range(1, 4):
            if group == 0:
                step = lax.rem(at_y + k, 4)
                other = at_z * 16 + step * 4 + at_x
            else:
                step = lax.rem(at_x + k, 4)
                other = at_z * 16 + at_y * 4 + step
            remote(
                second_out.at[group, step], second_in.at[group, k - 1],
                dirty_send.at[1, group], dirty_recv.at[1, group], other,
            ).start()

    def third_sum(group):
        wait_for(second_in.at[group], dirty_recv.at[1, group])
        total = second_out[group, at_y if group == 0 else at_x].astype(F32)
        for k in range(3):
            total += second_in[group, k].astype(F32)
        third_own[group] = total

    def third_stage():
        third_out[...] = third_own[1 - at_z].astype(BF16)
        remote(
            third_out, third_in, dirty_send.at[2, 0], dirty_recv.at[2, 0], lax.rem(me + 16, DEVICES)
        ).start()

    def hermitian_rows(f):
        for s in range(NP):
            grid_buf[s] = run_buf[last[f * NP + s, 0]].astype(BF16)

        def mirrored(r, c):
            return dot(mirror_rows, stack(grid_buf[c * 4 + 3 - r], grid_buf[c * 4 + (4 - r) % 4])).astype(BF16)

        def folded(own, rows, c):
            near, edge = rows[3 - c], rows[(4 - c) % 4]
            real = dot(lanes(near[:, :S], edge[:, :S]), mirror_cols)
            imag = dot(lanes(near[:, S:], edge[:, S:]), mirror_cols)
            return own.astype(F32) + lanes(real, -imag)

        middle = [grid_buf[c * 4 + 2, 0:ROWS, :] for c in range(4)]
        last_rows = [folded(middle[c], middle, c) for c in range(4)]
        blocks = []
        for r in range(2):
            rows = [mirrored(r, c) for c in range(4)]
            blocks.append([folded(grid_buf[c * 4 + r], rows, c).astype(BF16) for c in range(4)])
        tail_row = lax.broadcasted_iota(jnp.int32, (ROWS, 2 * S), 0)
        for r in range(2):
            next_rows = [blocks[1][c][0:ROWS].astype(F32) if r == 0 else last_rows[c] for c in range(4)]
            for c in range(4):
                after = (c + 1) % 4
                ends = contract(pick_ends, blocks[r][after], ((1,), (1,)))
                tail = jnp.where(
                    tail_row == 0, next_rows[c][0:1, :],
                    jnp.where(
                        tail_row == 1, lanes(ends[0:1, :], ends[1:2, :]),
                        jnp.where(tail_row == 2, next_rows[after][0:1, :], 0.0),
                    ),
                )
                first_out[f, r, c, 0:S, :] = blocks[r][c]
                first_out[f, r, c, S:EXT, :] = tail.astype(BF16)

    for f in (0, 2, 1, 3):
        hermitian_rows(f)
        first_stage(f)

    wait_for(cnt_in, recv_sems.at[4])
    counts = jnp.sum(cnt_in[...].astype(F32), axis=0)

    low = pl.multiple_of(row_block * S, S)

    def model_grid(stage):
        wait_for(column_buf.at[stage], recv_sems.at[2 * stage])
        half = column_buf[stage].reshape(P_SIZE, WIDE)
        edge = dot(half[:, 2 * S:], quarter_turn).astype(BF16)
        turned = lanes(half[:, S:2 * S], -half[:, :S], -edge)
        return dot(cs_ref[0, pl.ds(low, EXT), :], half) + dot(cs_ref[1, pl.ds(low, EXT), :], turned)

    def slot_model(grid):
        first = grid[:S, :2 * S]
        rows = dot(unfold_rows, grid).astype(BF16)
        second = lanes(
            dot(lanes(rows[:, :S], rows[:, 2 * S:]), mirror_cols),
            -dot(lanes(rows[:, S:2 * S], rows[:, 2 * S:]), far_cols),
        ).astype(BF16)
        for q, patch in enumerate((first, second)):
            operand = stack(patch, lanes(-patch[:, S:], patch[:, :S]))
            for w in range(WPLANES):
                part = dot(left_op[w * S:(w + 1) * S, :], operand)
                scale = counts[q, w:w + 1, :]
                b_buf[q * S:(q + 1) * S, w * 2 * S:(w + 1) * 2 * S] = (part * lanes(scale, scale)).astype(BF16)
        model = dot(b_buf[...], right_op[...])
        rows = dot(fold_rows, model[S:].astype(BF16)).astype(BF16)
        real, imag = dot(rows[:, :S], near_spread), dot(rows[:, S:], far_spread)
        mirrored = lanes(real[:, :S], -imag[:, :S], real[:, S:] - imag[:, S:])
        own = stack(lanes(model[:S], jnp.zeros((S, S), F32)), jnp.zeros((ROWS, WIDE), F32))
        return own + mirrored

    spread_buf[EXT:, :] = jnp.zeros((2 * S - EXT, WIDE), BF16)
    turn_pad = jnp.zeros((2 * S - EXT, WIDE), BF16)

    def column_transform(stage, values):
        values = values.astype(BF16)
        edge = dot(values[:, 2 * S:], quarter_turn).astype(BF16)
        turned = stack(lanes(-values[:, S:2 * S], values[:, :S], edge), turn_pad)
        spread_buf[:EXT, :] = values
        u_buf[stage] = (
            dot(cs_ref[0, :, pl.ds(low, 2 * S)], spread_buf[...]) + dot(cs_ref[1, :, pl.ds(low, 2 * S)], turned)
        ).astype(BF16)
        exchange_rows(stage)

    def image_rows(stage):
        wait_for(row_in.at[stage], recv_sems.at[2 * stage + 1])
        parts = [
            (row_in[stage, 2 * c].astype(F32) + row_in[stage, 2 * c + 1].astype(F32)).astype(BF16)
            for c in range(4)
        ]
        return dot(lanes(*parts), to_rows[...])

    column_transform(0, slot_model(model_grid(0).astype(BF16)))
    second_stage(0)
    second_stage(1)
    sky = (sky_ref[1].astype(F32) - (LOOP_GAIN * WEIGHT) * image_rows(0)).astype(BF16)
    half_buf[1] = dot(sky, to_cols[...]).astype(BF16)
    third_sum(0)
    third_sum(1)
    third_stage()
    exchange_columns(1)
    grid = model_grid(1)
    wait_for(third_in, dirty_recv.at[2, 0])
    dirty = third_own[at_z] + third_in[...].astype(F32)
    tail = dirty[S:].astype(BF16)
    ends = contract(tail[:, :S], put_real, ((0,), (0,))) + contract(tail[:, S:], put_imag, ((0,), (0,)))
    corner_row = lax.broadcasted_iota(jnp.int32, (ROWS, S), 0)
    corner_lane = lax.broadcasted_iota(jnp.int32, (ROWS, S), 1)
    corner = jnp.where(
        corner_row > 0, 0.0,
        jnp.where(
            corner_lane == 0, dirty[S + 2:S + 3, 0:1],
            jnp.where(corner_lane == 1, dirty[S + 2:S + 3, S:S + 1], 0.0),
        ),
    )
    grid += (0.5 * LOOP_GAIN * WEIGHT) * lanes(dirty, stack(ends, corner))
    model = slot_model(grid.astype(BF16))
    ext_row = lax.broadcasted_iota(jnp.int32, (EXT, 2 * S), 0)
    share = jnp.where(
        ext_row == 0, jnp.where(row_block == 0, 0.5, 1.0),
        jnp.where(ext_row < S, 1.0, jnp.where((ext_row == S) & (row_block == 1), 0.5, 0.0)),
    )
    column_transform(1, lanes(dirty * share - model[:, :2 * S], -model[:, 2 * S:]))
    out_ref[...] = image_rows(1) * WEIGHT

    for stage in range(2):
        wait_for(column_buf.at[stage, pl.ds(0, DEVICES - 1)], send_sems.at[2 * stage])
        wait_for(u_buf.at[stage, pl.ds(0, P_SIZE - ROWS), :], send_sems.at[2 * stage + 1])
    wait_for(cnt_in.at[pl.ds(0, DEVICES - 1)], send_sems.at[4])
    for f in range(F):
        wait_for(first_in.at[f], dirty_send.at[0, f])
    for group in range(2):
        wait_for(second_in.at[group], dirty_send.at[1, group])
    wait_for(third_in, dirty_send.at[2, 0])


def imaging(*operands):
    hbm = pl.BlockSpec(memory_space=pltpu.HBM)
    return pl.pallas_call(
        imaging_kernel,
        out_shape=jax.ShapeDtypeStruct((F * ROWS, P_SIZE), F32),
        in_specs=[hbm] * 9,
        out_specs=pl.BlockSpec(memory_space=pltpu.VMEM),
        scratch_shapes=[
            pltpu.SMEM((TILE_CAP,), jnp.int32),
            pltpu.SMEM((TILE_CAP,), jnp.int32),
            pltpu.SMEM((TILE_CAP,), jnp.int32),
            pltpu.SMEM((1,), jnp.int32),
            pltpu.VMEM((2, F * ROWS, P_SIZE), BF16),
            pltpu.VMEM((2, P_SIZE, P_SIZE), BF16),
            pltpu.VMEM((P_SIZE, P_SIZE), BF16),
            pltpu.VMEM((WPLANES, 2, S, S), BF16),
            pltpu.VMEM((TILE_CAP, 2, S, S), BF16),
            pltpu.VMEM((WPLANES, S, 2 * S), BF16),
            pltpu.VMEM((WPLANES, 2 * S, 2 * S), BF16),
            pltpu.VMEM((TILE_CAP + 1, S, 2 * S), F32),
            pltpu.VMEM((NP, S, 2 * S), BF16),
            pltpu.VMEM((4 * WIDE, P_SIZE), BF16),
            pltpu.VMEM((P_SIZE, 4 * WIDE), BF16),
            pltpu.VMEM((2, F * ROWS, 4 * WIDE), BF16),
            pltpu.VMEM((2, DEVICES, ROWS, WIDE), BF16),
            pltpu.VMEM((2, P_SIZE, WIDE), BF16),
            pltpu.VMEM((2, 8, F * ROWS, WIDE), BF16),
            pltpu.VMEM((DEVICES, 2, WPLANES, S), BF16),
            pltpu.VMEM((DEVICES, 2, WPLANES, S), BF16),
            pltpu.VMEM((WPLANES * S, 2 * S), BF16),
            pltpu.VMEM((WPLANES * 2 * S, 2 * S), BF16),
            pltpu.VMEM((2 * S, WPLANES * 2 * S), BF16),
            pltpu.VMEM((2 * S, WIDE), BF16),
            pltpu.VMEM((F, 2, 4, EXT, 2 * S), BF16),
            pltpu.VMEM((F, 3, 2, EXT, 2 * S), BF16),
            pltpu.VMEM((2, 4, EXT, 2 * S), BF16),
            pltpu.VMEM((2, 3, EXT, 2 * S), BF16),
            pltpu.VMEM((2, EXT, 2 * S), F32),
            pltpu.VMEM((EXT, 2 * S), BF16),
            pltpu.VMEM((EXT, 2 * S), BF16),
            pltpu.SemaphoreType.DMA((8,)),
            pltpu.SemaphoreType.DMA((CHUNKS,)),
            pltpu.SemaphoreType.DMA((5,)),
            pltpu.SemaphoreType.DMA((5,)),
            pltpu.SemaphoreType.DMA((3, F)),
            pltpu.SemaphoreType.DMA((3, F)),
        ],
        compiler_params=pltpu.CompilerParams(
            collective_id=0, has_side_effects=True, vmem_limit_bytes=56 << 20
        ),
        name="imaging",
    )(*operands)


def dft_tables():
    phases = np.outer(np.arange(P_SIZE), np.arange(P_SIZE)) % P_SIZE
    angles = phases * (2.0 * math.pi / P_SIZE)
    tables = np.stack([np.cos(angles), np.sin(angles)]) / math.sqrt(P_SIZE)
    edges = np.zeros((P_SIZE, 4, S))
    for c in range(4):
        edges[:, c, 0] = tables[0, :, (c + 1) % 4 * S]
        edges[:, c, 1] = -tables[1, :, (c + 1) % 4 * S]
    return tables.astype(BF16), edges.reshape(P_SIZE, P_SIZE).astype(BF16)


def local(model_input, w_kernels, visibilities, tile_facet, tile_patch, tile_wplane, tile_count):
    sky = model_input.reshape(2, F * ROWS, P_SIZE)
    cosines, edges = dft_tables()
    image = imaging(
        tile_facet, tile_patch, tile_wplane, tile_count,
        sky, jnp.asarray(cosines), jnp.asarray(edges), w_kernels, visibilities,
    )
    return image.reshape(F, ROWS, P_SIZE)


def solution(mesh):
    return jax.shard_map(
        local,
        mesh=mesh,
        in_specs=(
            P(None, "freq", "vis", None),
            P("freq", None, None, None),
            P(("freq", "vis"), None, None, None),
            P(("freq", "vis")),
            P(("freq", "vis")),
            P(("freq", "vis")),
            P(("freq", "vis")),
        ),
        out_specs=P("freq", "vis", None),
        check_vma=False,
    )
```

```python
import math

import jax
import jax.numpy as jnp
import numpy as np
from jax import lax
from jax.experimental import pallas as pl
from jax.experimental.pallas import tpu as pltpu
from jax.sharding import PartitionSpec as P

P_SIZE = 512
S = 128
F = 4
WPLANES = 16
TILE_CAP = 32
NP = 16
SLOTS = F * NP
DEVICES = 32
ROWS = P_SIZE // DEVICES
TILES = TILE_CAP * DEVICES
WEIGHT = math.sqrt(F * NP / TILES)
LOOP_GAIN = 0.5
MESH = pl.DeviceIdType.MESH
BF16 = jnp.bfloat16
F32 = jnp.float32
VIS_CHUNK = 4
CHUNKS = TILE_CAP // VIS_CHUNK
EXT = S + ROWS
WIDE = 3 * S


def dot(a, b):
    return lax.dot_general(a, b, (((1,), (0,)), ((), ())), preferred_element_type=F32)


def lanes(*parts):
    return jnp.concatenate(parts, axis=1)


def stack(*parts):
    return jnp.concatenate(parts, axis=0)


def owner(device):
    z, y, x = lax.div(device, 16), lax.rem(lax.div(device, 4), 4), lax.rem(device, 4)
    a, b = y + z * (x - y), x + z * (y - x)
    return 2 * z + lax.div(a, 2), lax.rem(a, 2), b


def static_owner(device):
    z, y, x = device // 16, device // 4 % 4, device % 4
    a, b = (x, y) if z else (y, x)
    return 2 * z + a // 2, a % 2, b


def slot_of(f, row, column):
    return f * NP + column * 4 + row


def where_equal(shape, rule):
    row = lax.broadcasted_iota(jnp.int32, shape, 0)
    column = lax.broadcasted_iota(jnp.int32, shape, 1)
    return rule(row, column).astype(BF16)


def one_if(condition):
    return jnp.where(condition, 1.0, 0.0)


def imaging_kernel(
    facet_hbm, patch_hbm, plane_hbm, count_hbm, sky_hbm, cs_hbm, edge_hbm, w_hbm, vis_hbm, out_ref,
    facet_ref, patch_ref, plane_ref, count_ref, sky_ref, cs_ref, edge_ref, w_ref, vis_buf,
    back_op, term_op, run_buf, grid_buf, to_rows, to_cols, half_buf, column_buf, u_buf, row_in,
    cnt_buf, left_op, right_op, b_buf, spread_buf,
    first_out, first_in, second_out, second_in, third_own, third_out, third_in,
    fold_buf, last_ref, load_sems, vis_sems, plane_sem, group_sem, send_sems, recv_sems, dirty_send, dirty_recv,
):
    me = lax.axis_index("vis")
    facet, row_block, column = owner(me)
    at_x, at_y, at_z = lax.rem(me, 4), lax.rem(lax.div(me, 4), 4), lax.div(me, 16)

    loads = [
        pltpu.make_async_copy(src, dst, load_sems.at[k])
        for k, (src, dst) in enumerate(
            (
                (facet_hbm, facet_ref), (patch_hbm, patch_ref), (plane_hbm, plane_ref), (count_hbm, count_ref),
                (w_hbm, w_ref), (cs_hbm, cs_ref), (sky_hbm, sky_ref), (edge_hbm, edge_ref),
            )
        )
    ]
    vis_loads = [
        pltpu.make_async_copy(
            vis_hbm.at[pl.ds(k * VIS_CHUNK, VIS_CHUNK)],
            vis_buf.at[pl.ds(k * VIS_CHUNK, VIS_CHUNK)],
            vis_sems.at[k],
        )
        for k in range(CHUNKS)
    ]
    for copy in loads[:5] + vis_loads + loads[5:]:
        copy.start()

    barrier = pltpu.get_barrier_semaphore()

    along_x = [at_z * 16 + at_y * 4 + lax.rem(at_x + k, 4) for k in range(1, 4)]
    along_y = [at_z * 16 + lax.rem(at_y + k, 4) * 4 + at_x for k in range(1, 4)]
    across = lax.rem(me + 16, DEVICES)

    def tell(semaphore, others):
        for other in others:
            pl.semaphore_signal(semaphore, inc=1, device_id={"vis": other}, device_id_type=MESH)

    tell(barrier, along_x + along_y + [across])

    def remote(src, dst, send, recv, other):
        return pltpu.make_async_remote_copy(
            src_ref=src, dst_ref=dst, send_sem=send, recv_sem=recv,
            device_id={"vis": other}, device_id_type=MESH,
        )

    def wait_for(ref, sem):
        pltpu.make_async_copy(ref, ref, sem).wait()

    def to_all(piece, place, index):
        @pl.loop(1, DEVICES)
        def _(k):
            other = lax.rem(me + k, DEVICES)
            remote(piece(other), place, send_sems.at[index], recv_sems.at[index], other).start()

        pltpu.make_async_copy(piece(me), place, recv_sems.at[index]).start()

    def exchange_columns(stage):
        width = WIDE - stage * S

        def piece(other):
            f, _, c = owner(other)
            return half_buf.at[
                stage,
                pl.ds(pl.multiple_of(f * ROWS, ROWS), ROWS),
                pl.ds(pl.multiple_of(c * WIDE, S), width),
            ]

        to_all(piece, column_buf.at[stage, me, :, pl.ds(0, width)], 2 * stage)

    def exchange_rows():
        def piece(other):
            return u_buf.at[pl.ds(pl.multiple_of(other * ROWS, ROWS), ROWS), :]

        place = row_in.at[column * 2 + row_block, pl.ds(pl.multiple_of(facet * ROWS, ROWS), ROWS), :]
        to_all(piece, place, 1)

    for copy in loads[:4]:
        copy.wait()

    lane = lax.broadcasted_iota(jnp.int32, (1, S), 1)
    tile = lax.broadcasted_iota(jnp.int32, (TILE_CAP, S), 0)
    slot_row = jnp.full((1, S), SLOTS, jnp.int32)
    plane_row = jnp.full((1, S), WPLANES, jnp.int32)
    slot_column = jnp.full((TILE_CAP, S), SLOTS, jnp.int32)
    for t in range(TILE_CAP):
        patch = patch_ref[t]
        slot = facet_ref[t] * NP + lax.rem(patch, 4) * 4 + lax.div(patch, 4)
        slot = jnp.where(t < count_ref[0], slot, SLOTS)
        slot_row = jnp.where(lane == t, slot, slot_row)
        plane_row = jnp.where(lane == t, plane_ref[t], plane_row)
        slot_column = jnp.where(tile == t, slot, slot_column)
    tile_lane = lax.broadcasted_iota(jnp.int32, (TILE_CAP, S), 1)
    before = jnp.max(
        jnp.where((slot_column == slot_row) & (tile_lane < tile), tile_lane, -1), axis=1, keepdims=True
    )
    slot_lane = lax.broadcasted_iota(jnp.int32, (SLOTS, S), 1)
    member = lax.broadcasted_iota(jnp.int32, (SLOTS, S), 0) == slot_row
    last = jnp.max(jnp.where(member, slot_lane, -1), axis=1, keepdims=True)
    before = jnp.where(before < 0, TILE_CAP, before)
    last = jnp.where(last < 0, TILE_CAP, last)
    for s in range(SLOTS):
        last_ref[s] = last[s, 0]

    in_plane = jnp.where(
        lax.broadcasted_iota(jnp.int32, (WPLANES, S), 0) == plane_row, 1.0, 0.0
    )
    in_slot = jnp.where(member, 1.0, 0.0)
    in_plane = in_plane.astype(BF16)
    lane_row = lax.broadcasted_iota(jnp.int32, (S, S), 0)

    def contract(a, b, dims):
        return lax.dot_general(a, b, (dims, ((), ())), preferred_element_type=F32)

    for f in range(F):
        for c in range(4):
            match = jnp.zeros((S, S), F32)
            for k, (r, q) in enumerate(((0, 0), (0, 1), (1, 0), (1, 1))):
                s = slot_of(f, 3 - r, 3 - c) if q else slot_of(f, r, c)
                match = jnp.where(lane_row == 4 + k, in_slot[s:s + 1, :], match)
            cnt_buf[f * ROWS:(f + 1) * ROWS, c * S:(c + 1) * S] = contract(in_plane, match.astype(BF16), ((1,), (1,)))

    loads[4].wait()

    @pl.loop(0, WPLANES)
    def _(w):
        real, imag = w_ref[w, 0], w_ref[w, 1]
        back_op[w] = lanes(real.T, imag.T)
        term_op[w] = stack(lanes(real, -imag), lanes(imag, real))

    run_buf[TILE_CAP] = jnp.zeros((S, 2 * S), F32)
    for k in range(CHUNKS):
        vis_loads[k].wait()
        for t in range(k * VIS_CHUNK, (k + 1) * VIS_CHUNK):
            plane = plane_ref[t]
            real, imag = vis_buf[t, 0], vis_buf[t, 1]
            half = dot(lanes(real, imag), term_op[plane])
            half_real, half_imag = half[:, :S].astype(BF16), half[:, S:].astype(BF16)
            term = dot(
                back_op[plane], stack(lanes(half_real, half_imag), lanes(half_imag, -half_real))
            )
            run_buf[t] = term + run_buf[before[t, 0]]
        if k == CHUNKS // 2 - 1:
            pl.semaphore_wait(barrier, 7)
            tell(plane_sem, along_y)
    pl.semaphore_wait(plane_sem, 3)
    tell(group_sem, [across])

    loads[5].wait()
    loads[7].wait()
    for c in range(4):
        at, low = c * 2 * S, c * S
        to_cols[:, at:at + S] = cs_ref[0, :, low:low + S]
        to_cols[:, at + S:at + 2 * S] = -cs_ref[1, :, low:low + S]
    loads[6].wait()
    for cycle in range(2):
        half = dot(sky_ref[cycle], to_cols[...])
        for c in range(4):
            half_buf[cycle, :, c * WIDE:c * WIDE + 2 * S] = half[:, c * 2 * S:(c + 1) * 2 * S].astype(BF16)
    extra = cnt_buf[...] + dot(sky_ref[0], edge_ref[...]) + pltpu.roll(dot(sky_ref[1], edge_ref[...]), 2, 1)
    for c in range(4):
        half_buf[0, :, c * WIDE + 2 * S:(c + 1) * WIDE] = extra[:, c * S:(c + 1) * S].astype(BF16)

    mirror_rows = where_equal(
        (S, 2 * S), lambda i, k: one_if(((k == S - i) & (i > 0)) | ((k == S) & (i == 0)))
    )
    mirror_cols = where_equal(
        (2 * S, S), lambda k, j: one_if(((k == S - j) & (j > 0)) | ((k == S) & (j == 0)))
    )
    far_cols = where_equal(
        (2 * S, S), lambda k, j: one_if(((k == S - j) & (j > 0)) | ((k == S + 1) & (j == 0)))
    )
    near_spread = where_equal(
        (S, 2 * S), lambda j, k: one_if(((k == S - j) & (j > 0)) | ((k == S) & (j == 0)))
    )
    far_spread = where_equal(
        (S, 2 * S), lambda j, k: one_if(((k == S - j) & (j > 0)) | ((k == S + 1) & (j == 0)))
    )
    unfold_rows = where_equal((S, EXT), lambda i, k: one_if(k == S - i))
    fold_rows = where_equal((EXT, S), lambda k, i: one_if(k == S - i))
    quarter_turn = where_equal(
        (S, S), lambda i, j: one_if((i == 0) & (j == 1)) - one_if((i == 1) & (j == 0))
    )
    pick_ends = where_equal(
        (ROWS, 2 * S), lambda i, k: one_if(((i == 0) & (k == 0)) | ((i == 1) & (k == S)))
    )
    pick_edge = [
        where_equal((S, S), lambda i, j: one_if((i == 2 * cycle + j) & (j < 2))) for cycle in range(2)
    ]
    put_real = where_equal((ROWS, S), lambda i, j: one_if((i == 1) & (j == 0)))
    put_imag = where_equal((ROWS, S), lambda i, j: one_if((i == 1) & (j == 1)))

    def first_stage(f):
        turn = lax.div(f, 2)
        for k in range(1, 4):
            step = lax.rem(at_x + turn * (at_y - at_x) + k, 4)
            x, y = at_x + (1 - turn) * (step - at_x), at_y + turn * (step - at_y)
            remote(
                first_out.at[f, :, step], first_in.at[f, k - 1], dirty_send.at[0, f], dirty_recv.at[0, f],
                at_z * 16 + y * 4 + x,
            ).start()

    def second_stage(group):
        for f in (2 * group, 2 * group + 1):
            wait_for(first_in.at[f], dirty_recv.at[0, f])
            total = first_out[f, :, at_x if group == 0 else at_y].astype(F32)
            for k in range(3):
                total += first_in[f, k].astype(F32)
            second_out[group, 2 * (f % 2):2 * (f % 2) + 2] = total.astype(BF16)
        for k in range(1, 4):
            if group == 0:
                step = lax.rem(at_y + k, 4)
                other = at_z * 16 + step * 4 + at_x
            else:
                step = lax.rem(at_x + k, 4)
                other = at_z * 16 + at_y * 4 + step
            remote(
                second_out.at[group, step], second_in.at[group, k - 1],
                dirty_send.at[1, group], dirty_recv.at[1, group], other,
            ).start()

    def third_sum(group):
        wait_for(second_in.at[group], dirty_recv.at[1, group])
        total = second_out[group, at_y if group == 0 else at_x].astype(F32)
        for k in range(3):
            total += second_in[group, k].astype(F32)
        third_own[group] = total

    def third_stage():
        third_out[...] = third_own[1 - at_z].astype(BF16)
        remote(
            third_out, third_in, dirty_send.at[2, 0], dirty_recv.at[2, 0], lax.rem(me + 16, DEVICES)
        ).start()

    def hermitian_rows(f, model=None):
        for s in range(NP):
            grid_buf[s] = run_buf[last_ref[f * NP + s]].astype(BF16)
        if model is not None:
            for q, s in enumerate((column * 4 + row_block, (3 - column) * 4 + 3 - row_block)):
                grid_buf[s] = (run_buf[last_ref[f * NP + s]] - model[q * S:(q + 1) * S]).astype(BF16)

        def mirrored(r, c):
            return dot(mirror_rows, stack(grid_buf[c * 4 + 3 - r], grid_buf[c * 4 + (4 - r) % 4])).astype(BF16)

        def folded(own, rows, c):
            near, edge = rows[3 - c], rows[(4 - c) % 4]
            real = dot(lanes(near[:, :S], edge[:, :S]), mirror_cols)
            imag = dot(lanes(near[:, S:], edge[:, S:]), mirror_cols)
            return own.astype(F32) + lanes(real, -imag)

        middle = [grid_buf[c * 4 + 2, 0:ROWS, :] for c in range(4)]
        last_rows = [folded(middle[c], middle, c) for c in range(4)]
        blocks = []
        for r in range(2):
            rows = [mirrored(r, c) for c in range(4)]
            blocks.append([folded(grid_buf[c * 4 + r], rows, c).astype(BF16) for c in range(4)])
        tail_row = lax.broadcasted_iota(jnp.int32, (ROWS, 2 * S), 0)
        for r in range(2):
            next_rows = [blocks[1][c][0:ROWS].astype(F32) if r == 0 else last_rows[c] for c in range(4)]
            for c in range(4):
                after = (c + 1) % 4
                ends = contract(pick_ends, blocks[r][after], ((1,), (1,)))
                tail = jnp.where(
                    tail_row == 0, next_rows[c][0:1, :],
                    jnp.where(
                        tail_row == 1, lanes(ends[0:1, :], ends[1:2, :]),
                        jnp.where(tail_row == 2, next_rows[after][0:1, :], 0.0),
                    ),
                )
                first_out[f, r, c, 0:S, :] = blocks[r][c]
                first_out[f, r, c, S:EXT, :] = tail.astype(BF16)

    turn, part = lax.div(facet, 2), lax.rem(facet, 2)
    others = (2 * (1 - turn) + part, 2 * turn + 1 - part, 2 * (1 - turn) + 1 - part)
    pl.semaphore_wait(group_sem, 1)
    exchange_columns(0)
    exchange_columns(1)
    for f in others:
        hermitian_rows(f)
        first_stage(f)

    @pl.loop(0, WPLANES)
    def _(w):
        real, imag = w_ref[w, 0], w_ref[w, 1]
        gram = dot(back_op[w], stack(lanes(real, imag), lanes(imag, -real))).astype(BF16)
        gram_real, gram_imag = gram[:, :S], gram[:, S:]
        left_op[pl.ds(w * S, S), :] = gram
        right_op[pl.ds(w * 2 * S, S), :] = lanes(gram_real, -gram_imag)
        right_op[pl.ds(w * 2 * S + S, S), :] = lanes(gram_imag, gram_real)

    low = pl.multiple_of(row_block * S, S)

    def model_grid(stage):
        half = column_buf[stage, :, :, 0:2 * S].reshape(P_SIZE, 2 * S)
        extra = column_buf[0, :, :, 2 * S:].reshape(P_SIZE, S)
        edge = dot(extra, pick_edge[stage]).astype(BF16)
        edge_turned = dot(edge, quarter_turn).astype(BF16)
        turned = lanes(half[:, S:], -half[:, :S], -edge_turned)
        return dot(cs_ref[0, pl.ds(low, EXT), :], lanes(half, edge)) + dot(cs_ref[1, pl.ds(low, EXT), :], turned)

    def slot_model(grid):
        first = grid[:S, :2 * S]
        rows = dot(unfold_rows, grid).astype(BF16)
        second = lanes(
            dot(lanes(rows[:, :S], rows[:, 2 * S:]), mirror_cols),
            -dot(lanes(rows[:, S:2 * S], rows[:, 2 * S:]), far_cols),
        ).astype(BF16)
        for q, patch in enumerate((first, second)):
            operand = stack(patch, lanes(-patch[:, S:], patch[:, :S]))
            for w in range(WPLANES):
                part = dot(left_op[w * S:(w + 1) * S, :], operand)
                b_buf[q * S:(q + 1) * S, w * 2 * S:(w + 1) * 2 * S] = (part * counts[w:w + 1, q:q + 1]).astype(BF16)
        model = dot(b_buf[...], right_op[...])
        rows = dot(fold_rows, model[S:].astype(BF16)).astype(BF16)
        real, imag = dot(rows[:, :S], near_spread), dot(rows[:, S:], far_spread)
        mirrored = lanes(real[:, :S], -imag[:, :S], real[:, S:] - imag[:, S:])
        own = stack(lanes(model[:S], jnp.zeros((S, S), F32)), jnp.zeros((ROWS, WIDE), F32))
        return model, own + mirrored

    spread_buf[EXT:, :] = jnp.zeros((2 * S - EXT, WIDE), BF16)
    turn_pad = jnp.zeros((2 * S - EXT, WIDE), BF16)

    def column_transform(values):
        values = values.astype(BF16)
        edge = dot(values[:, 2 * S:], quarter_turn).astype(BF16)
        turned = stack(lanes(-values[:, S:2 * S], values[:, :S], edge), turn_pad)
        spread_buf[:EXT, :] = values
        u_buf[...] = (
            dot(cs_ref[0, :, pl.ds(low, 2 * S)], spread_buf[...]) + dot(cs_ref[1, :, pl.ds(low, 2 * S)], turned)
        ).astype(BF16)
        exchange_rows()

    def image_rows():
        wait_for(row_in, recv_sems.at[1])
        parts = [
            (row_in[2 * c].astype(F32) + row_in[2 * c + 1].astype(F32)).astype(BF16)
            for c in range(4)
        ]
        return dot(lanes(*parts), to_rows[...])

    wait_for(column_buf.at[0], recv_sems.at[0])
    counts = jnp.sum(column_buf[0, :, :, 2 * S:].astype(F32), axis=0)
    counts = jnp.where(row_block == 0, counts[:, 4:6], counts[:, 6:8])
    model, folded_model = slot_model(model_grid(0).astype(BF16))
    fold_buf[...] = folded_model
    hermitian_rows(facet, model)
    first_stage(facet)
    row = lax.broadcasted_iota(jnp.int32, (S, P_SIZE), 0)
    for c in range(4):
        at, first, edge = c * WIDE, c * S, (c + 1) % 4 * S
        to_rows[at:at + S, :] = cs_ref[0, first:first + S, :]
        to_rows[at + S:at + 2 * S, :] = -cs_ref[1, first:first + S, :]
        cosine_row = cs_ref[0, edge:edge + 1, :].astype(F32)
        sine_row = cs_ref[1, edge:edge + 1, :].astype(F32)
        to_rows[at + 2 * S:at + WIDE, :] = jnp.where(
            row == 0, cosine_row, jnp.where(row == 1, -sine_row, 0.0)
        ).astype(BF16)
    second_stage(0)
    second_stage(1)
    wait_for(column_buf.at[1, :, :, pl.ds(0, 2 * S)], recv_sems.at[2])
    grid = model_grid(1)
    third_sum(0)
    third_sum(1)
    third_stage()
    wait_for(third_in, dirty_recv.at[2, 0])
    dirty = third_own[at_z] + third_in[...].astype(F32)
    tail = dirty[S:].astype(BF16)
    ends = contract(tail[:, :S], put_real, ((0,), (0,))) + contract(tail[:, S:], put_imag, ((0,), (0,)))
    corner_row = lax.broadcasted_iota(jnp.int32, (ROWS, S), 0)
    corner_lane = lax.broadcasted_iota(jnp.int32, (ROWS, S), 1)
    corner = jnp.where(
        corner_row > 0, 0.0,
        jnp.where(
            corner_lane == 0, dirty[S + 2:S + 3, 0:1],
            jnp.where(corner_lane == 1, dirty[S + 2:S + 3, S:S + 1], 0.0),
        ),
    )
    grid += (0.5 * LOOP_GAIN * WEIGHT) * lanes(dirty, stack(ends, corner))
    _, folded_model = slot_model(grid.astype(BF16))
    ext_row = lax.broadcasted_iota(jnp.int32, (EXT, 2 * S), 0)
    share = jnp.where(
        ext_row == 0, jnp.where(row_block == 0, 0.5, 1.0),
        jnp.where(ext_row < S, 1.0, jnp.where((ext_row == S) & (row_block == 1), 0.5, 0.0)),
    )
    model = fold_buf[...] - folded_model
    column_transform(lanes(dirty * share + model[:, :2 * S], model[:, 2 * S:]))
    out_ref[...] = image_rows() * WEIGHT

    wait_for(column_buf.at[0, pl.ds(0, DEVICES - 1)], send_sems.at[0])
    wait_for(column_buf.at[1, pl.ds(0, DEVICES - 1), :, pl.ds(0, 2 * S)], send_sems.at[2])
    wait_for(u_buf.at[pl.ds(0, P_SIZE - ROWS), :], send_sems.at[1])
    for f in range(F):
        wait_for(first_in.at[f], dirty_send.at[0, f])
    for group in range(2):
        wait_for(second_in.at[group], dirty_send.at[1, group])
    wait_for(third_in, dirty_send.at[2, 0])


def imaging(*operands):
    hbm = pl.BlockSpec(memory_space=pltpu.HBM)
    return pl.pallas_call(
        imaging_kernel,
        out_shape=jax.ShapeDtypeStruct((F * ROWS, P_SIZE), F32),
        in_specs=[hbm] * 9,
        out_specs=pl.BlockSpec(memory_space=pltpu.VMEM),
        scratch_shapes=[
            pltpu.SMEM((TILE_CAP,), jnp.int32),
            pltpu.SMEM((TILE_CAP,), jnp.int32),
            pltpu.SMEM((TILE_CAP,), jnp.int32),
            pltpu.SMEM((1,), jnp.int32),
            pltpu.VMEM((2, F * ROWS, P_SIZE), BF16),
            pltpu.VMEM((2, P_SIZE, P_SIZE), BF16),
            pltpu.VMEM((P_SIZE, P_SIZE), BF16),
            pltpu.VMEM((WPLANES, 2, S, S), BF16),
            pltpu.VMEM((TILE_CAP, 2, S, S), BF16),
            pltpu.VMEM((WPLANES, S, 2 * S), BF16),
            pltpu.VMEM((WPLANES, 2 * S, 2 * S), BF16),
            pltpu.VMEM((TILE_CAP + 1, S, 2 * S), F32),
            pltpu.VMEM((NP, S, 2 * S), BF16),
            pltpu.VMEM((4 * WIDE, P_SIZE), BF16),
            pltpu.VMEM((P_SIZE, 2 * P_SIZE), BF16),
            pltpu.VMEM((2, F * ROWS, 4 * WIDE), BF16),
            pltpu.VMEM((2, DEVICES, ROWS, WIDE), BF16),
            pltpu.VMEM((P_SIZE, WIDE), BF16),
            pltpu.VMEM((8, F * ROWS, WIDE), BF16),
            pltpu.VMEM((F * ROWS, P_SIZE), F32),
            pltpu.VMEM((WPLANES * S, 2 * S), BF16),
            pltpu.VMEM((WPLANES * 2 * S, 2 * S), BF16),
            pltpu.VMEM((2 * S, WPLANES * 2 * S), BF16),
            pltpu.VMEM((2 * S, WIDE), BF16),
            pltpu.VMEM((F, 2, 4, EXT, 2 * S), BF16),
            pltpu.VMEM((F, 3, 2, EXT, 2 * S), BF16),
            pltpu.VMEM((2, 4, EXT, 2 * S), BF16),
            pltpu.VMEM((2, 3, EXT, 2 * S), BF16),
            pltpu.VMEM((2, EXT, 2 * S), F32),
            pltpu.VMEM((EXT, 2 * S), BF16),
            pltpu.VMEM((EXT, 2 * S), BF16),
            pltpu.VMEM((EXT, WIDE), F32),
            pltpu.SMEM((SLOTS,), jnp.int32),
            pltpu.SemaphoreType.DMA((8,)),
            pltpu.SemaphoreType.DMA((CHUNKS,)),
            pltpu.SemaphoreType.REGULAR,
            pltpu.SemaphoreType.REGULAR,
            pltpu.SemaphoreType.DMA((3,)),
            pltpu.SemaphoreType.DMA((3,)),
            pltpu.SemaphoreType.DMA((3, F)),
            pltpu.SemaphoreType.DMA((3, F)),
        ],
        compiler_params=pltpu.CompilerParams(
            collective_id=0, has_side_effects=True, vmem_limit_bytes=56 << 20
        ),
        name="imaging",
    )(*operands)


def dft_tables():
    phases = np.outer(np.arange(P_SIZE), np.arange(P_SIZE)) % P_SIZE
    angles = phases * (2.0 * math.pi / P_SIZE)
    tables = np.stack([np.cos(angles), np.sin(angles)]) / math.sqrt(P_SIZE)
    edges = np.zeros((P_SIZE, 4, S))
    for c in range(4):
        edges[:, c, 0] = tables[0, :, (c + 1) % 4 * S]
        edges[:, c, 1] = -tables[1, :, (c + 1) % 4 * S]
    return tables.astype(BF16), edges.reshape(P_SIZE, P_SIZE).astype(BF16)


def local(model_input, w_kernels, visibilities, tile_facet, tile_patch, tile_wplane, tile_count):
    sky = model_input.reshape(2, F * ROWS, P_SIZE)
    cosines, edges = dft_tables()
    image = imaging(
        tile_facet, tile_patch, tile_wplane, tile_count,
        sky, jnp.asarray(cosines), jnp.asarray(edges), w_kernels, visibilities,
    )
    return image.reshape(F, ROWS, P_SIZE)


def solution(mesh):
    return jax.shard_map(
        local,
        mesh=mesh,
        in_specs=(
            P(None, "freq", "vis", None),
            P("freq", None, None, None),
            P(("freq", "vis"), None, None, None),
            P(("freq", "vis")),
            P(("freq", "vis")),
            P(("freq", "vis")),
            P(("freq", "vis")),
        ),
        out_specs=P("freq", "vis", None),
        check_vma=False,
    )
```

```python
import math

import jax
import jax.numpy as jnp
import numpy as np
from jax import lax
from jax.experimental import pallas as pl
from jax.experimental.pallas import tpu as pltpu
from jax.sharding import PartitionSpec as P

P_SIZE = 512
S = 128
F = 4
WPLANES = 16
TILE_CAP = 32
NP = 16
SLOTS = F * NP
DEVICES = 32
ROWS = P_SIZE // DEVICES
TILES = TILE_CAP * DEVICES
WEIGHT = math.sqrt(F * NP / TILES)
LOOP_GAIN = 0.5
MESH = pl.DeviceIdType.MESH
BF16 = jnp.bfloat16
F32 = jnp.float32
VIS_CHUNK = 4
CHUNKS = TILE_CAP // VIS_CHUNK
EXT = S + ROWS
WIDE = 3 * S


def dot(a, b):
    return lax.dot_general(a, b, (((1,), (0,)), ((), ())), preferred_element_type=F32)


def lanes(*parts):
    return jnp.concatenate(parts, axis=1)


def stack(*parts):
    return jnp.concatenate(parts, axis=0)


def owner(device):
    z, y, x = lax.div(device, 16), lax.rem(lax.div(device, 4), 4), lax.rem(device, 4)
    a, b = y + z * (x - y), x + z * (y - x)
    return 2 * z + lax.div(a, 2), lax.rem(a, 2), b


def static_owner(device):
    z, y, x = device // 16, device // 4 % 4, device % 4
    a, b = (x, y) if z else (y, x)
    return 2 * z + a // 2, a % 2, b


def slot_of(f, row, column):
    return f * NP + column * 4 + row


def where_equal(shape, rule):
    row = lax.broadcasted_iota(jnp.int32, shape, 0)
    column = lax.broadcasted_iota(jnp.int32, shape, 1)
    return rule(row, column).astype(BF16)


def one_if(condition):
    return jnp.where(condition, 1.0, 0.0)


def imaging_kernel(
    facet_hbm, patch_hbm, plane_hbm, count_hbm, sky_hbm, cs_hbm, edge_hbm, w_hbm, vis_hbm, out_ref,
    facet_ref, patch_ref, plane_ref, count_ref, sky_ref, cs_ref, edge_ref, w_ref, vis_buf,
    back_op, term_op, run_buf, grid_buf, to_rows, to_cols, half_buf, column_buf, u_buf, row_in,
    cnt_buf, left_op, right_op, b_buf, spread_buf,
    first_out, first_in, second_out, second_in,
    fold_buf, last_ref, load_sems, vis_sems, send_sems, recv_sems, dirty_send, dirty_recv,
):
    me = lax.axis_index("vis")
    facet, row_block, column = owner(me)
    at_x, at_y, at_z = lax.rem(me, 4), lax.rem(lax.div(me, 4), 4), lax.div(me, 16)

    barrier = pltpu.get_barrier_semaphore()

    @pl.loop(1, DEVICES)
    def _(k):
        other = lax.rem(me + k, DEVICES)
        pl.semaphore_signal(barrier, inc=1, device_id={"vis": other}, device_id_type=MESH)

    loads = [
        pltpu.make_async_copy(src, dst, load_sems.at[k])
        for k, (src, dst) in enumerate(
            (
                (facet_hbm, facet_ref), (patch_hbm, patch_ref), (plane_hbm, plane_ref), (count_hbm, count_ref),
                (w_hbm, w_ref), (cs_hbm, cs_ref), (sky_hbm, sky_ref), (edge_hbm, edge_ref),
            )
        )
    ]
    vis_loads = [
        pltpu.make_async_copy(
            vis_hbm.at[pl.ds(k * VIS_CHUNK, VIS_CHUNK)],
            vis_buf.at[pl.ds(k * VIS_CHUNK, VIS_CHUNK)],
            vis_sems.at[k],
        )
        for k in range(CHUNKS)
    ]
    for copy in loads[:4] + loads[5:] + loads[4:5] + vis_loads:
        copy.start()


    def remote(src, dst, send, recv, other):
        return pltpu.make_async_remote_copy(
            src_ref=src, dst_ref=dst, send_sem=send, recv_sem=recv,
            device_id={"vis": other}, device_id_type=MESH,
        )

    def wait_for(ref, sem):
        pltpu.make_async_copy(ref, ref, sem).wait()

    def to_all(piece, place, index):
        @pl.loop(1, DEVICES)
        def _(k):
            other = lax.rem(me + k, DEVICES)
            remote(piece(other), place, send_sems.at[index], recv_sems.at[index], other).start()

        pltpu.make_async_copy(piece(me), place, recv_sems.at[index]).start()

    def exchange_columns(stage):
        width = WIDE - stage * S

        def piece(other):
            f, _, c = owner(other)
            return half_buf.at[
                stage,
                pl.ds(pl.multiple_of(f * ROWS, ROWS), ROWS),
                pl.ds(pl.multiple_of(c * WIDE, S), width),
            ]

        to_all(piece, column_buf.at[stage, me, :, pl.ds(0, width)], 2 * stage)

    def exchange_rows():
        def piece(other):
            return u_buf.at[pl.ds(pl.multiple_of(other * ROWS, ROWS), ROWS), :]

        place = row_in.at[column * 2 + row_block, pl.ds(pl.multiple_of(facet * ROWS, ROWS), ROWS), :]
        to_all(piece, place, 1)

    for copy in loads[:4]:
        copy.wait()

    lane = lax.broadcasted_iota(jnp.int32, (1, S), 1)
    tile = lax.broadcasted_iota(jnp.int32, (TILE_CAP, S), 0)
    slot_row = jnp.full((1, S), SLOTS, jnp.int32)
    plane_row = jnp.full((1, S), WPLANES, jnp.int32)
    slot_column = jnp.full((TILE_CAP, S), SLOTS, jnp.int32)
    for t in range(TILE_CAP):
        patch = patch_ref[t]
        slot = facet_ref[t] * NP + lax.rem(patch, 4) * 4 + lax.div(patch, 4)
        slot = jnp.where(t < count_ref[0], slot, SLOTS)
        slot_row = jnp.where(lane == t, slot, slot_row)
        plane_row = jnp.where(lane == t, plane_ref[t], plane_row)
        slot_column = jnp.where(tile == t, slot, slot_column)
    tile_lane = lax.broadcasted_iota(jnp.int32, (TILE_CAP, S), 1)
    before = jnp.max(
        jnp.where((slot_column == slot_row) & (tile_lane < tile), tile_lane, -1), axis=1, keepdims=True
    )
    slot_lane = lax.broadcasted_iota(jnp.int32, (SLOTS, S), 1)
    member = lax.broadcasted_iota(jnp.int32, (SLOTS, S), 0) == slot_row
    last = jnp.max(jnp.where(member, slot_lane, -1), axis=1, keepdims=True)
    before = jnp.where(before < 0, TILE_CAP, before)
    last = jnp.where(last < 0, TILE_CAP, last)
    for s in range(SLOTS):
        last_ref[s] = last[s, 0]

    in_plane = jnp.where(
        lax.broadcasted_iota(jnp.int32, (WPLANES, S), 0) == plane_row, 1.0, 0.0
    )
    in_slot = jnp.where(member, 1.0, 0.0)
    in_plane = in_plane.astype(BF16)
    lane_row = lax.broadcasted_iota(jnp.int32, (S, S), 0)

    def contract(a, b, dims):
        return lax.dot_general(a, b, (dims, ((), ())), preferred_element_type=F32)

    for f in range(F):
        for c in range(4):
            match = jnp.zeros((S, S), F32)
            for k, (r, q) in enumerate(((0, 0), (0, 1), (1, 0), (1, 1))):
                s = slot_of(f, 3 - r, 3 - c) if q else slot_of(f, r, c)
                match = jnp.where(lane_row == 4 + k, in_slot[s:s + 1, :], match)
            cnt_buf[f * ROWS:(f + 1) * ROWS, c * S:(c + 1) * S] = contract(in_plane, match.astype(BF16), ((1,), (1,)))

    loads[5].wait()
    loads[7].wait()
    for c in range(4):
        at, low = c * 2 * S, c * S
        to_cols[:, at:at + S] = cs_ref[0, :, low:low + S]
        to_cols[:, at + S:at + 2 * S] = -cs_ref[1, :, low:low + S]
    loads[6].wait()
    for cycle in range(2):
        half = dot(sky_ref[cycle], to_cols[...])
        for c in range(4):
            half_buf[cycle, :, c * WIDE:c * WIDE + 2 * S] = half[:, c * 2 * S:(c + 1) * 2 * S].astype(BF16)
    extra = cnt_buf[...] + dot(sky_ref[0], edge_ref[...]) + pltpu.roll(dot(sky_ref[1], edge_ref[...]), 2, 1)
    for c in range(4):
        half_buf[0, :, c * WIDE + 2 * S:(c + 1) * WIDE] = extra[:, c * S:(c + 1) * S].astype(BF16)

    loads[4].wait()

    @pl.loop(0, WPLANES)
    def _(w):
        real, imag = w_ref[w, 0], w_ref[w, 1]
        back_op[w] = lanes(real.T, imag.T)
        term_op[w] = stack(lanes(real, -imag), lanes(imag, real))

    run_buf[TILE_CAP] = jnp.zeros((S, 2 * S), F32)
    for k in range(CHUNKS):
        vis_loads[k].wait()
        for t in range(k * VIS_CHUNK, (k + 1) * VIS_CHUNK):
            plane = plane_ref[t]
            real, imag = vis_buf[t, 0], vis_buf[t, 1]
            half = dot(lanes(real, imag), term_op[plane])
            half_real, half_imag = half[:, :S].astype(BF16), half[:, S:].astype(BF16)
            term = dot(
                back_op[plane], stack(lanes(half_real, half_imag), lanes(half_imag, -half_real))
            )
            run_buf[t] = term + run_buf[before[t, 0]]
        if k == 6:
            pl.semaphore_wait(barrier, DEVICES - 1)
            exchange_columns(0)

    mirror_rows = where_equal(
        (S, 2 * S), lambda i, k: one_if(((k == S - i) & (i > 0)) | ((k == S) & (i == 0)))
    )
    mirror_cols = where_equal(
        (2 * S, S), lambda k, j: one_if(((k == S - j) & (j > 0)) | ((k == S) & (j == 0)))
    )
    far_cols = where_equal(
        (2 * S, S), lambda k, j: one_if(((k == S - j) & (j > 0)) | ((k == S + 1) & (j == 0)))
    )
    near_spread = where_equal(
        (S, 2 * S), lambda j, k: one_if(((k == S - j) & (j > 0)) | ((k == S) & (j == 0)))
    )
    far_spread = where_equal(
        (S, 2 * S), lambda j, k: one_if(((k == S - j) & (j > 0)) | ((k == S + 1) & (j == 0)))
    )
    unfold_rows = where_equal((S, EXT), lambda i, k: one_if(k == S - i))
    fold_rows = where_equal((EXT, S), lambda k, i: one_if(k == S - i))
    quarter_turn = where_equal(
        (S, S), lambda i, j: one_if((i == 0) & (j == 1)) - one_if((i == 1) & (j == 0))
    )
    pick_ends = where_equal(
        (ROWS, 2 * S), lambda i, k: one_if(((i == 0) & (k == 0)) | ((i == 1) & (k == S)))
    )
    pick_edge = [
        where_equal((S, S), lambda i, j: one_if((i == 2 * cycle + j) & (j < 2))) for cycle in range(2)
    ]
    put_real = where_equal((ROWS, S), lambda i, j: one_if((i == 1) & (j == 0)))
    put_imag = where_equal((ROWS, S), lambda i, j: one_if((i == 1) & (j == 1)))

    def first_stage(f):
        turn = lax.div(f, 2)
        for k in range(1, 4):
            step = lax.rem(at_x + turn * (at_y - at_x) + k, 4)
            x, y = at_x + (1 - turn) * (step - at_x), at_y + turn * (step - at_y)
            remote(
                first_out.at[f, :, step], first_in.at[f, k - 1], dirty_send.at[0, f], dirty_recv.at[0, f],
                at_z * 16 + y * 4 + x,
            ).start()

    def second_stage(f):
        wait_for(first_in.at[f], dirty_recv.at[0, f])
        turn, part = lax.div(f, 2), lax.rem(f, 2)
        total = first_out[f, :, at_x + turn * (at_y - at_x)].astype(F32)
        for k in range(3):
            total += first_in[f, k].astype(F32)
        second_out[f] = total.astype(BF16)
        place = second_in.at[at_z * 4 + at_y + turn * (at_x - at_y)]
        for r in range(2):
            a = 2 * part + r
            other = turn * 16 + (a + turn * (at_y - a)) * 4 + at_x + turn * (a - at_x)

            @pl.when(other == me)
            def _():
                pltpu.make_async_copy(second_out.at[f, r], place, dirty_recv.at[1, 0]).start()

            @pl.when(other != me)
            def _():
                remote(second_out.at[f, r], place, dirty_send.at[1, 0], dirty_recv.at[1, 0], other).start()

    def hermitian_rows(f, model=None):
        for s in range(NP):
            grid_buf[s] = run_buf[last_ref[f * NP + s]].astype(BF16)
        if model is not None:
            for q, s in enumerate((column * 4 + row_block, (3 - column) * 4 + 3 - row_block)):
                grid_buf[s] = (run_buf[last_ref[f * NP + s]] - model[q * S:(q + 1) * S]).astype(BF16)

        def mirrored(r, c):
            return dot(mirror_rows, stack(grid_buf[c * 4 + 3 - r], grid_buf[c * 4 + (4 - r) % 4])).astype(BF16)

        def folded(own, rows, c):
            near, edge = rows[3 - c], rows[(4 - c) % 4]
            real = dot(lanes(near[:, :S], edge[:, :S]), mirror_cols)
            imag = dot(lanes(near[:, S:], edge[:, S:]), mirror_cols)
            return own.astype(F32) + lanes(real, -imag)

        middle = [grid_buf[c * 4 + 2, 0:ROWS, :] for c in range(4)]
        last_rows = [folded(middle[c], middle, c) for c in range(4)]
        blocks = []
        for r in range(2):
            rows = [mirrored(r, c) for c in range(4)]
            blocks.append([folded(grid_buf[c * 4 + r], rows, c).astype(BF16) for c in range(4)])
        tail_row = lax.broadcasted_iota(jnp.int32, (ROWS, 2 * S), 0)
        for r in range(2):
            next_rows = [blocks[1][c][0:ROWS].astype(F32) if r == 0 else last_rows[c] for c in range(4)]
            for c in range(4):
                after = (c + 1) % 4
                ends = contract(pick_ends, blocks[r][after], ((1,), (1,)))
                tail = jnp.where(
                    tail_row == 0, next_rows[c][0:1, :],
                    jnp.where(
                        tail_row == 1, lanes(ends[0:1, :], ends[1:2, :]),
                        jnp.where(tail_row == 2, next_rows[after][0:1, :], 0.0),
                    ),
                )
                first_out[f, r, c, 0:S, :] = blocks[r][c]
                first_out[f, r, c, S:EXT, :] = tail.astype(BF16)

    turn, part = lax.div(facet, 2), lax.rem(facet, 2)
    others = (2 * (1 - turn) + part, 2 * turn + 1 - part, 2 * (1 - turn) + 1 - part)
    for f in others[:2]:
        hermitian_rows(f)
        first_stage(f)
    hermitian_rows(others[2])

    @pl.loop(0, WPLANES)
    def _(w):
        real, imag = w_ref[w, 0], w_ref[w, 1]
        gram = dot(back_op[w], stack(lanes(real, imag), lanes(imag, -real))).astype(BF16)
        gram_real, gram_imag = gram[:, :S], gram[:, S:]
        left_op[pl.ds(w * S, S), :] = gram
        right_op[pl.ds(w * 2 * S, S), :] = lanes(gram_real, -gram_imag)
        right_op[pl.ds(w * 2 * S + S, S), :] = lanes(gram_imag, gram_real)

    low = pl.multiple_of(row_block * S, S)

    def model_grid(stage):
        half = column_buf[stage, :, :, 0:2 * S].reshape(P_SIZE, 2 * S)
        extra = column_buf[0, :, :, 2 * S:].reshape(P_SIZE, S)
        edge = dot(extra, pick_edge[stage]).astype(BF16)
        edge_turned = dot(edge, quarter_turn).astype(BF16)
        turned = lanes(half[:, S:], -half[:, :S], -edge_turned)
        return dot(cs_ref[0, pl.ds(low, EXT), :], lanes(half, edge)) + dot(cs_ref[1, pl.ds(low, EXT), :], turned)

    def slot_model(grid):
        first = grid[:S, :2 * S]
        rows = dot(unfold_rows, grid).astype(BF16)
        second = lanes(
            dot(lanes(rows[:, :S], rows[:, 2 * S:]), mirror_cols),
            -dot(lanes(rows[:, S:2 * S], rows[:, 2 * S:]), far_cols),
        ).astype(BF16)
        for q, patch in enumerate((first, second)):
            operand = stack(patch, lanes(-patch[:, S:], patch[:, :S]))
            for w in range(WPLANES):
                part = dot(left_op[w * S:(w + 1) * S, :], operand)
                b_buf[q * S:(q + 1) * S, w * 2 * S:(w + 1) * 2 * S] = (part * counts[w:w + 1, q:q + 1]).astype(BF16)
        model = dot(b_buf[...], right_op[...])
        rows = dot(fold_rows, model[S:].astype(BF16)).astype(BF16)
        real, imag = dot(rows[:, :S], near_spread), dot(rows[:, S:], far_spread)
        mirrored = lanes(real[:, :S], -imag[:, :S], real[:, S:] - imag[:, S:])
        own = stack(lanes(model[:S], jnp.zeros((S, S), F32)), jnp.zeros((ROWS, WIDE), F32))
        return model, own + mirrored

    spread_buf[EXT:, :] = jnp.zeros((2 * S - EXT, WIDE), BF16)
    turn_pad = jnp.zeros((2 * S - EXT, WIDE), BF16)

    def column_transform(values):
        values = values.astype(BF16)
        edge = dot(values[:, 2 * S:], quarter_turn).astype(BF16)
        turned = stack(lanes(-values[:, S:2 * S], values[:, :S], edge), turn_pad)
        spread_buf[:EXT, :] = values
        u_buf[...] = (
            dot(cs_ref[0, :, pl.ds(low, 2 * S)], spread_buf[...]) + dot(cs_ref[1, :, pl.ds(low, 2 * S)], turned)
        ).astype(BF16)
        exchange_rows()

    def image_rows():
        wait_for(row_in, recv_sems.at[1])
        parts = [
            (row_in[2 * c].astype(F32) + row_in[2 * c + 1].astype(F32)).astype(BF16)
            for c in range(4)
        ]
        return dot(lanes(*parts), to_rows[...])

    wait_for(column_buf.at[0], recv_sems.at[0])
    counts = jnp.sum(column_buf[0, :, :, 2 * S:].astype(F32), axis=0)
    counts = jnp.where(row_block == 0, counts[:, 4:6], counts[:, 6:8])
    model, folded_model = slot_model(model_grid(0).astype(BF16))
    fold_buf[...] = folded_model
    hermitian_rows(facet, model)
    first_stage(others[2])
    first_stage(facet)
    exchange_columns(1)
    row = lax.broadcasted_iota(jnp.int32, (S, P_SIZE), 0)
    for c in range(4):
        at, first, edge = c * WIDE, c * S, (c + 1) % 4 * S
        to_rows[at:at + S, :] = cs_ref[0, first:first + S, :]
        to_rows[at + S:at + 2 * S, :] = -cs_ref[1, first:first + S, :]
        cosine_row = cs_ref[0, edge:edge + 1, :].astype(F32)
        sine_row = cs_ref[1, edge:edge + 1, :].astype(F32)
        to_rows[at + 2 * S:at + WIDE, :] = jnp.where(
            row == 0, cosine_row, jnp.where(row == 1, -sine_row, 0.0)
        ).astype(BF16)
    for f in others + (facet,):
        second_stage(f)
    wait_for(column_buf.at[1, :, :, pl.ds(0, 2 * S)], recv_sems.at[2])
    grid = model_grid(1)
    wait_for(second_in, dirty_recv.at[1, 0])
    dirty = second_in[0].astype(F32)
    for k in range(1, 8):
        dirty += second_in[k].astype(F32)
    tail = dirty[S:].astype(BF16)
    ends = contract(tail[:, :S], put_real, ((0,), (0,))) + contract(tail[:, S:], put_imag, ((0,), (0,)))
    corner_row = lax.broadcasted_iota(jnp.int32, (ROWS, S), 0)
    corner_lane = lax.broadcasted_iota(jnp.int32, (ROWS, S), 1)
    corner = jnp.where(
        corner_row > 0, 0.0,
        jnp.where(
            corner_lane == 0, dirty[S + 2:S + 3, 0:1],
            jnp.where(corner_lane == 1, dirty[S + 2:S + 3, S:S + 1], 0.0),
        ),
    )
    grid += (0.5 * LOOP_GAIN * WEIGHT) * lanes(dirty, stack(ends, corner))
    _, folded_model = slot_model(grid.astype(BF16))
    ext_row = lax.broadcasted_iota(jnp.int32, (EXT, 2 * S), 0)
    share = jnp.where(
        ext_row == 0, jnp.where(row_block == 0, 0.5, 1.0),
        jnp.where(ext_row < S, 1.0, jnp.where((ext_row == S) & (row_block == 1), 0.5, 0.0)),
    )
    model = fold_buf[...] - folded_model
    column_transform(lanes(dirty * share + model[:, :2 * S], model[:, 2 * S:]))
    out_ref[...] = image_rows() * WEIGHT

    wait_for(column_buf.at[0, pl.ds(0, DEVICES - 1)], send_sems.at[0])
    wait_for(column_buf.at[1, pl.ds(0, DEVICES - 1), :, pl.ds(0, 2 * S)], send_sems.at[2])
    wait_for(u_buf.at[pl.ds(0, P_SIZE - ROWS), :], send_sems.at[1])
    for f in range(F):
        wait_for(first_in.at[f], dirty_send.at[0, f])
    wait_for(second_in.at[pl.ds(0, 7)], dirty_send.at[1, 0])


def imaging(*operands):
    hbm = pl.BlockSpec(memory_space=pltpu.HBM)
    return pl.pallas_call(
        imaging_kernel,
        out_shape=jax.ShapeDtypeStruct((F * ROWS, P_SIZE), F32),
        in_specs=[hbm] * 9,
        out_specs=pl.BlockSpec(memory_space=pltpu.VMEM),
        scratch_shapes=[
            pltpu.SMEM((TILE_CAP,), jnp.int32),
            pltpu.SMEM((TILE_CAP,), jnp.int32),
            pltpu.SMEM((TILE_CAP,), jnp.int32),
            pltpu.SMEM((1,), jnp.int32),
            pltpu.VMEM((2, F * ROWS, P_SIZE), BF16),
            pltpu.VMEM((2, P_SIZE, P_SIZE), BF16),
            pltpu.VMEM((P_SIZE, P_SIZE), BF16),
            pltpu.VMEM((WPLANES, 2, S, S), BF16),
            pltpu.VMEM((TILE_CAP, 2, S, S), BF16),
            pltpu.VMEM((WPLANES, S, 2 * S), BF16),
            pltpu.VMEM((WPLANES, 2 * S, 2 * S), BF16),
            pltpu.VMEM((TILE_CAP + 1, S, 2 * S), F32),
            pltpu.VMEM((NP, S, 2 * S), BF16),
            pltpu.VMEM((4 * WIDE, P_SIZE), BF16),
            pltpu.VMEM((P_SIZE, 2 * P_SIZE), BF16),
            pltpu.VMEM((2, F * ROWS, 4 * WIDE), BF16),
            pltpu.VMEM((2, DEVICES, ROWS, WIDE), BF16),
            pltpu.VMEM((P_SIZE, WIDE), BF16),
            pltpu.VMEM((8, F * ROWS, WIDE), BF16),
            pltpu.VMEM((F * ROWS, P_SIZE), F32),
            pltpu.VMEM((WPLANES * S, 2 * S), BF16),
            pltpu.VMEM((WPLANES * 2 * S, 2 * S), BF16),
            pltpu.VMEM((2 * S, WPLANES * 2 * S), BF16),
            pltpu.VMEM((2 * S, WIDE), BF16),
            pltpu.VMEM((F, 2, 4, EXT, 2 * S), BF16),
            pltpu.VMEM((F, 3, 2, EXT, 2 * S), BF16),
            pltpu.VMEM((F, 2, EXT, 2 * S), BF16),
            pltpu.VMEM((8, EXT, 2 * S), BF16),
            pltpu.VMEM((EXT, WIDE), F32),
            pltpu.SMEM((SLOTS,), jnp.int32),
            pltpu.SemaphoreType.DMA((8,)),
            pltpu.SemaphoreType.DMA((CHUNKS,)),
            pltpu.SemaphoreType.DMA((3,)),
            pltpu.SemaphoreType.DMA((3,)),
            pltpu.SemaphoreType.DMA((2, F)),
            pltpu.SemaphoreType.DMA((2, F)),
        ],
        compiler_params=pltpu.CompilerParams(
            collective_id=0, has_side_effects=True, vmem_limit_bytes=56 << 20
        ),
        name="imaging",
    )(*operands)


def dft_tables():
    phases = np.outer(np.arange(P_SIZE), np.arange(P_SIZE)) % P_SIZE
    angles = phases * (2.0 * math.pi / P_SIZE)
    tables = np.stack([np.cos(angles), np.sin(angles)]) / math.sqrt(P_SIZE)
    edges = np.zeros((P_SIZE, 4, S))
    for c in range(4):
        edges[:, c, 0] = tables[0, :, (c + 1) % 4 * S]
        edges[:, c, 1] = -tables[1, :, (c + 1) % 4 * S]
    return tables.astype(BF16), edges.reshape(P_SIZE, P_SIZE).astype(BF16)


def local(model_input, w_kernels, visibilities, tile_facet, tile_patch, tile_wplane, tile_count):
    sky = model_input.reshape(2, F * ROWS, P_SIZE)
    cosines, edges = dft_tables()
    image = imaging(
        tile_facet, tile_patch, tile_wplane, tile_count,
        sky, jnp.asarray(cosines), jnp.asarray(edges), w_kernels, visibilities,
    )
    return image.reshape(F, ROWS, P_SIZE)


def solution(mesh):
    return jax.shard_map(
        local,
        mesh=mesh,
        in_specs=(
            P(None, "freq", "vis", None),
            P("freq", None, None, None),
            P(("freq", "vis"), None, None, None),
            P(("freq", "vis")),
            P(("freq", "vis")),
            P(("freq", "vis")),
            P(("freq", "vis")),
        ),
        out_specs=P("freq", "vis", None),
        check_vma=False,
    )
```

```python
import math

import jax
import jax.numpy as jnp
import numpy as np
from jax import lax
from jax.experimental import pallas as pl
from jax.experimental.pallas import tpu as pltpu
from jax.sharding import PartitionSpec as P

P_SIZE = 512
S = 128
F = 4
WPLANES = 16
TILE_CAP = 32
NP = 16
SLOTS = F * NP
DEVICES = 32
ROWS = P_SIZE // DEVICES
TILES = TILE_CAP * DEVICES
WEIGHT = math.sqrt(F * NP / TILES)
LOOP_GAIN = 0.5
MESH = pl.DeviceIdType.MESH
BF16 = jnp.bfloat16
F32 = jnp.float32
VIS_CHUNK = 4
CHUNKS = TILE_CAP // VIS_CHUNK
EXT = S + ROWS
WIDE = 3 * S


def dot(a, b):
    return lax.dot_general(a, b, (((1,), (0,)), ((), ())), preferred_element_type=F32)


def lanes(*parts):
    return jnp.concatenate(parts, axis=1)


def stack(*parts):
    return jnp.concatenate(parts, axis=0)


def owner(device):
    z, y, x = lax.div(device, 16), lax.rem(lax.div(device, 4), 4), lax.rem(device, 4)
    a, b = y + z * (x - y), x + z * (y - x)
    return 2 * z + lax.div(a, 2), lax.rem(a, 2), b


def static_owner(device):
    z, y, x = device // 16, device // 4 % 4, device % 4
    a, b = (x, y) if z else (y, x)
    return 2 * z + a // 2, a % 2, b


def slot_of(f, row, column):
    return f * NP + column * 4 + row


def where_equal(shape, rule):
    row = lax.broadcasted_iota(jnp.int32, shape, 0)
    column = lax.broadcasted_iota(jnp.int32, shape, 1)
    return rule(row, column).astype(BF16)


def one_if(condition):
    return jnp.where(condition, 1.0, 0.0)


def imaging_kernel(
    facet_hbm, patch_hbm, plane_hbm, count_hbm, sky_hbm, cs_hbm, edge_hbm, w_hbm, vis_hbm, out_ref,
    facet_ref, patch_ref, plane_ref, count_ref, sky_ref, cs_ref, edge_ref, w_ref, vis_buf,
    back_op, term_op, run_buf, grid_buf, to_rows, to_cols, half_buf, column_buf, u_buf, row_in,
    cnt_buf, left_op, right_op, b_buf, spread_buf,
    first_out, first_in, second_out, second_in,
    fold_buf, last_ref, load_sems, vis_sems, send_sems, recv_sems, dirty_send, dirty_recv,
):
    me = lax.axis_index("vis")
    facet, row_block, column = owner(me)
    at_x, at_y, at_z = lax.rem(me, 4), lax.rem(lax.div(me, 4), 4), lax.div(me, 16)

    barrier = pltpu.get_barrier_semaphore()

    @pl.loop(1, DEVICES)
    def _(k):
        other = lax.rem(me + k, DEVICES)
        pl.semaphore_signal(barrier, inc=1, device_id={"vis": other}, device_id_type=MESH)

    loads = [
        pltpu.make_async_copy(src, dst, load_sems.at[k])
        for k, (src, dst) in enumerate(
            (
                (facet_hbm, facet_ref), (patch_hbm, patch_ref), (plane_hbm, plane_ref), (count_hbm, count_ref),
                (w_hbm, w_ref), (cs_hbm, cs_ref), (sky_hbm, sky_ref), (edge_hbm, edge_ref),
            )
        )
    ]
    vis_loads = [
        pltpu.make_async_copy(
            vis_hbm.at[pl.ds(k * VIS_CHUNK, VIS_CHUNK)],
            vis_buf.at[pl.ds(k * VIS_CHUNK, VIS_CHUNK)],
            vis_sems.at[k],
        )
        for k in range(CHUNKS)
    ]
    for copy in loads[:4] + loads[5:] + loads[4:5] + vis_loads:
        copy.start()


    def remote(src, dst, send, recv, other):
        return pltpu.make_async_remote_copy(
            src_ref=src, dst_ref=dst, send_sem=send, recv_sem=recv,
            device_id={"vis": other}, device_id_type=MESH,
        )

    def wait_for(ref, sem):
        pltpu.make_async_copy(ref, ref, sem).wait()

    def to_all(piece, place, index):
        @pl.loop(1, DEVICES)
        def _(k):
            other = lax.rem(me + k, DEVICES)
            remote(piece(other), place, send_sems.at[index], recv_sems.at[index], other).start()

        pltpu.make_async_copy(piece(me), place, recv_sems.at[index]).start()

    def exchange_columns(stage):
        width = WIDE - stage * S

        def piece(other):
            f, _, c = owner(other)
            return half_buf.at[
                stage,
                pl.ds(pl.multiple_of(f * ROWS, ROWS), ROWS),
                pl.ds(pl.multiple_of(c * WIDE, S), width),
            ]

        to_all(piece, column_buf.at[stage, me, :, pl.ds(0, width)], 2 * stage)

    def exchange_rows():
        def piece(other):
            return u_buf.at[pl.ds(pl.multiple_of(other * ROWS, ROWS), ROWS), :]

        place = row_in.at[column * 2 + row_block, pl.ds(pl.multiple_of(facet * ROWS, ROWS), ROWS), :]
        to_all(piece, place, 1)

    for copy in loads[:4]:
        copy.wait()

    lane = lax.broadcasted_iota(jnp.int32, (1, S), 1)
    tile = lax.broadcasted_iota(jnp.int32, (TILE_CAP, S), 0)
    slot_row = jnp.full((1, S), SLOTS, jnp.int32)
    plane_row = jnp.full((1, S), WPLANES, jnp.int32)
    slot_column = jnp.full((TILE_CAP, S), SLOTS, jnp.int32)
    for t in range(TILE_CAP):
        patch = patch_ref[t]
        slot = facet_ref[t] * NP + lax.rem(patch, 4) * 4 + lax.div(patch, 4)
        slot = jnp.where(t < count_ref[0], slot, SLOTS)
        slot_row = jnp.where(lane == t, slot, slot_row)
        plane_row = jnp.where(lane == t, plane_ref[t], plane_row)
        slot_column = jnp.where(tile == t, slot, slot_column)
    tile_lane = lax.broadcasted_iota(jnp.int32, (TILE_CAP, S), 1)
    before = jnp.max(
        jnp.where((slot_column == slot_row) & (tile_lane < tile), tile_lane, -1), axis=1, keepdims=True
    )
    slot_lane = lax.broadcasted_iota(jnp.int32, (SLOTS, S), 1)
    member = lax.broadcasted_iota(jnp.int32, (SLOTS, S), 0) == slot_row
    last = jnp.max(jnp.where(member, slot_lane, -1), axis=1, keepdims=True)
    before = jnp.where(before < 0, TILE_CAP, before)
    last = jnp.where(last < 0, TILE_CAP, last)
    for s in range(SLOTS):
        last_ref[s] = last[s, 0]

    in_plane = jnp.where(
        lax.broadcasted_iota(jnp.int32, (WPLANES, S), 0) == plane_row, 1.0, 0.0
    )
    in_slot = jnp.where(member, 1.0, 0.0)
    in_plane = in_plane.astype(BF16)
    lane_row = lax.broadcasted_iota(jnp.int32, (S, S), 0)

    def contract(a, b, dims):
        return lax.dot_general(a, b, (dims, ((), ())), preferred_element_type=F32)

    for f in range(F):
        for c in range(4):
            match = jnp.zeros((S, S), F32)
            for k, (r, q) in enumerate(((0, 0), (0, 1), (1, 0), (1, 1))):
                s = slot_of(f, 3 - r, 3 - c) if q else slot_of(f, r, c)
                match = jnp.where(lane_row == 4 + k, in_slot[s:s + 1, :], match)
            cnt_buf[f * ROWS:(f + 1) * ROWS, c * S:(c + 1) * S] = contract(in_plane, match.astype(BF16), ((1,), (1,)))

    loads[5].wait()
    loads[7].wait()
    for c in range(4):
        at, low = c * 2 * S, c * S
        to_cols[:, at:at + S] = cs_ref[0, :, low:low + S]
        to_cols[:, at + S:at + 2 * S] = -cs_ref[1, :, low:low + S]
    loads[6].wait()
    for cycle in range(2):
        half = dot(sky_ref[cycle], to_cols[...])
        for c in range(4):
            half_buf[cycle, :, c * WIDE:c * WIDE + 2 * S] = half[:, c * 2 * S:(c + 1) * 2 * S].astype(BF16)
    extra = cnt_buf[...] + dot(sky_ref[0], edge_ref[...]) + pltpu.roll(dot(sky_ref[1], edge_ref[...]), 2, 1)
    for c in range(4):
        half_buf[0, :, c * WIDE + 2 * S:(c + 1) * WIDE] = extra[:, c * S:(c + 1) * S].astype(BF16)

    loads[4].wait()

    @pl.loop(0, WPLANES)
    def _(w):
        real, imag = w_ref[w, 0], w_ref[w, 1]
        back_op[w] = lanes(real.T, imag.T)
        term_op[w] = stack(lanes(real, -imag), lanes(imag, real))

    run_buf[TILE_CAP] = jnp.zeros((S, 2 * S), F32)
    for k in range(CHUNKS):
        vis_loads[k].wait()
        for t in range(k * VIS_CHUNK, (k + 1) * VIS_CHUNK):
            plane = plane_ref[t]
            real, imag = vis_buf[t, 0], vis_buf[t, 1]
            half = dot(lanes(real, imag), term_op[plane])
            half_real, half_imag = half[:, :S].astype(BF16), half[:, S:].astype(BF16)
            term = dot(
                back_op[plane], stack(lanes(half_real, half_imag), lanes(half_imag, -half_real))
            )
            run_buf[t] = term + run_buf[before[t, 0]]
        if k == 6:
            pl.semaphore_wait(barrier, DEVICES - 1)
            exchange_columns(0)

    mirror_rows = where_equal(
        (S, 2 * S), lambda i, k: one_if(((k == S - i) & (i > 0)) | ((k == S) & (i == 0)))
    )
    mirror_cols = where_equal(
        (2 * S, S), lambda k, j: one_if(((k == S - j) & (j > 0)) | ((k == S) & (j == 0)))
    )
    far_cols = where_equal(
        (2 * S, S), lambda k, j: one_if(((k == S - j) & (j > 0)) | ((k == S + 1) & (j == 0)))
    )
    near_spread = where_equal(
        (S, 2 * S), lambda j, k: one_if(((k == S - j) & (j > 0)) | ((k == S) & (j == 0)))
    )
    far_spread = where_equal(
        (S, 2 * S), lambda j, k: one_if(((k == S - j) & (j > 0)) | ((k == S + 1) & (j == 0)))
    )
    unfold_rows = where_equal((S, EXT), lambda i, k: one_if(k == S - i))
    fold_rows = where_equal((EXT, S), lambda k, i: one_if(k == S - i))
    quarter_turn = where_equal(
        (S, S), lambda i, j: one_if((i == 0) & (j == 1)) - one_if((i == 1) & (j == 0))
    )
    pick_ends = where_equal(
        (ROWS, 2 * S), lambda i, k: one_if(((i == 0) & (k == 0)) | ((i == 1) & (k == S)))
    )
    pick_edge = [
        where_equal((S, S), lambda i, j: one_if((i == 2 * cycle + j) & (j < 2))) for cycle in range(2)
    ]
    put_real = where_equal((ROWS, S), lambda i, j: one_if((i == 1) & (j == 0)))
    put_imag = where_equal((ROWS, S), lambda i, j: one_if((i == 1) & (j == 1)))

    def first_stage(f):
        turn = lax.div(f, 2)
        for k in range(1, 4):
            step = lax.rem(at_x + turn * (at_y - at_x) + k, 4)
            x, y = at_x + (1 - turn) * (step - at_x), at_y + turn * (step - at_y)
            remote(
                first_out.at[f, :, step], first_in.at[f, k - 1], dirty_send.at[0, f], dirty_recv.at[0, f],
                at_z * 16 + y * 4 + x,
            ).start()

    def second_stage(f):
        wait_for(first_in.at[f], dirty_recv.at[0, f])
        turn, part = lax.div(f, 2), lax.rem(f, 2)
        total = first_out[f, :, at_x + turn * (at_y - at_x)].astype(F32)
        for k in range(3):
            total += first_in[f, k].astype(F32)
        second_out[f] = total.astype(BF16)
        place = second_in.at[at_z * 4 + at_y + turn * (at_x - at_y)]
        for r in range(2):
            a = 2 * part + r
            other = turn * 16 + (a + turn * (at_y - a)) * 4 + at_x + turn * (a - at_x)

            @pl.when(other == me)
            def _():
                pltpu.make_async_copy(second_out.at[f, r], place, dirty_recv.at[1, 0]).start()

            @pl.when(other != me)
            def _():
                remote(second_out.at[f, r], place, dirty_send.at[1, 0], dirty_recv.at[1, 0], other).start()

    def hermitian_rows(f, model=None):
        for s in range(NP):
            grid_buf[s] = run_buf[last_ref[f * NP + s]].astype(BF16)
        if model is not None:
            for q, s in enumerate((column * 4 + row_block, (3 - column) * 4 + 3 - row_block)):
                grid_buf[s] = (run_buf[last_ref[f * NP + s]] - model[q * S:(q + 1) * S]).astype(BF16)

        def mirrored(r, c):
            return dot(mirror_rows, stack(grid_buf[c * 4 + 3 - r], grid_buf[c * 4 + (4 - r) % 4])).astype(BF16)

        def folded(own, rows, c):
            near, edge = rows[3 - c], rows[(4 - c) % 4]
            real = dot(lanes(near[:, :S], edge[:, :S]), mirror_cols)
            imag = dot(lanes(near[:, S:], edge[:, S:]), mirror_cols)
            return own.astype(F32) + lanes(real, -imag)

        middle = [grid_buf[c * 4 + 2, 0:ROWS, :] for c in range(4)]
        last_rows = [folded(middle[c], middle, c) for c in range(4)]
        blocks = []
        for r in range(2):
            rows = [mirrored(r, c) for c in range(4)]
            blocks.append([folded(grid_buf[c * 4 + r], rows, c).astype(BF16) for c in range(4)])
        tail_row = lax.broadcasted_iota(jnp.int32, (ROWS, 2 * S), 0)
        for r in range(2):
            next_rows = [blocks[1][c][0:ROWS].astype(F32) if r == 0 else last_rows[c] for c in range(4)]
            for c in range(4):
                after = (c + 1) % 4
                ends = contract(pick_ends, blocks[r][after], ((1,), (1,)))
                tail = jnp.where(
                    tail_row == 0, next_rows[c][0:1, :],
                    jnp.where(
                        tail_row == 1, lanes(ends[0:1, :], ends[1:2, :]),
                        jnp.where(tail_row == 2, next_rows[after][0:1, :], 0.0),
                    ),
                )
                first_out[f, r, c, 0:S, :] = blocks[r][c]
                first_out[f, r, c, S:EXT, :] = tail.astype(BF16)

    turn, part = lax.div(facet, 2), lax.rem(facet, 2)
    others = (2 * (1 - turn) + part, 2 * turn + 1 - part, 2 * (1 - turn) + 1 - part)
    for f in others[:2]:
        hermitian_rows(f)
        first_stage(f)
    hermitian_rows(others[2])

    @pl.loop(0, WPLANES)
    def _(w):
        real, imag = w_ref[w, 0], w_ref[w, 1]
        gram = dot(back_op[w], stack(lanes(real, imag), lanes(imag, -real))).astype(BF16)
        gram_real, gram_imag = gram[:, :S], gram[:, S:]
        left_op[pl.ds(w * S, S), :] = gram
        right_op[pl.ds(w * 2 * S, S), :] = lanes(gram_real, -gram_imag)
        right_op[pl.ds(w * 2 * S + S, S), :] = lanes(gram_imag, gram_real)

    low = pl.multiple_of(row_block * S, S)

    def model_grid(stage):
        half = column_buf[stage, :, :, 0:2 * S].reshape(P_SIZE, 2 * S)
        extra = column_buf[0, :, :, 2 * S:].reshape(P_SIZE, S)
        edge = dot(extra, pick_edge[stage]).astype(BF16)
        edge_turned = dot(edge, quarter_turn).astype(BF16)
        turned = lanes(half[:, S:], -half[:, :S], -edge_turned)
        return dot(cs_ref[0, pl.ds(low, EXT), :], lanes(half, edge)) + dot(cs_ref[1, pl.ds(low, EXT), :], turned)

    def slot_model(grid):
        first = grid[:S, :2 * S]
        rows = dot(unfold_rows, grid).astype(BF16)
        second = lanes(
            dot(lanes(rows[:, :S], rows[:, 2 * S:]), mirror_cols),
            -dot(lanes(rows[:, S:2 * S], rows[:, 2 * S:]), far_cols),
        ).astype(BF16)
        for q, patch in enumerate((first, second)):
            operand = stack(patch, lanes(-patch[:, S:], patch[:, :S]))
            for w in range(WPLANES):
                part = dot(left_op[w * S:(w + 1) * S, :], operand)
                b_buf[q * S:(q + 1) * S, w * 2 * S:(w + 1) * 2 * S] = (part * counts[w:w + 1, q:q + 1]).astype(BF16)
        model = dot(b_buf[...], right_op[...])
        rows = dot(fold_rows, model[S:].astype(BF16)).astype(BF16)
        real, imag = dot(rows[:, :S], near_spread), dot(rows[:, S:], far_spread)
        mirrored = lanes(real[:, :S], -imag[:, :S], real[:, S:] - imag[:, S:])
        own = stack(lanes(model[:S], jnp.zeros((S, S), F32)), jnp.zeros((ROWS, WIDE), F32))
        return model, own + mirrored

    spread_buf[EXT:, :] = jnp.zeros((2 * S - EXT, WIDE), BF16)
    turn_pad = jnp.zeros((2 * S - EXT, WIDE), BF16)

    def column_transform(values):
        values = values.astype(BF16)
        edge = dot(values[:, 2 * S:], quarter_turn).astype(BF16)
        turned = stack(lanes(-values[:, S:2 * S], values[:, :S], edge), turn_pad)
        spread_buf[:EXT, :] = values
        u_buf[...] = (
            dot(cs_ref[0, :, pl.ds(low, 2 * S)], spread_buf[...]) + dot(cs_ref[1, :, pl.ds(low, 2 * S)], turned)
        ).astype(BF16)
        exchange_rows()

    def image_rows():
        wait_for(row_in, recv_sems.at[1])
        parts = []
        edge = jnp.zeros((F * ROWS, S), F32)
        for c in range(4):
            both = row_in[2 * c].astype(F32) + row_in[2 * c + 1].astype(F32)
            parts.append(both[:, :2 * S].astype(BF16))
            ends = both[:, 2 * S:]
            edge += pltpu.roll(ends, 2 * c, 1) if c else ends
        parts.append(edge.astype(BF16))
        return dot(lanes(*parts), to_rows[...])

    wait_for(column_buf.at[0], recv_sems.at[0])
    counts = jnp.sum(column_buf[0, :, :, 2 * S:].astype(F32), axis=0)
    counts = jnp.where(row_block == 0, counts[:, 4:6], counts[:, 6:8])
    model, folded_model = slot_model(model_grid(0).astype(BF16))
    fold_buf[...] = folded_model
    hermitian_rows(facet, model)
    first_stage(others[2])
    first_stage(facet)
    exchange_columns(1)
    row = lax.broadcasted_iota(jnp.int32, (S, P_SIZE), 0)
    edge_rows = jnp.zeros((S, P_SIZE), F32)
    for c in range(4):
        at, first, edge = c * 2 * S, c * S, (c + 1) % 4 * S
        to_rows[at:at + S, :] = cs_ref[0, first:first + S, :]
        to_rows[at + S:at + 2 * S, :] = -cs_ref[1, first:first + S, :]
        cosine_row = cs_ref[0, edge:edge + 1, :].astype(F32)
        sine_row = cs_ref[1, edge:edge + 1, :].astype(F32)
        edge_rows = jnp.where(row == 2 * c, cosine_row, jnp.where(row == 2 * c + 1, -sine_row, edge_rows))
    to_rows[2 * P_SIZE:, :] = edge_rows.astype(BF16)
    for f in others + (facet,):
        second_stage(f)
    wait_for(column_buf.at[1, :, :, pl.ds(0, 2 * S)], recv_sems.at[2])
    grid = model_grid(1)
    wait_for(second_in, dirty_recv.at[1, 0])
    dirty = second_in[0].astype(F32)
    for k in range(1, 8):
        dirty += second_in[k].astype(F32)
    tail = dirty[S:].astype(BF16)
    ends = contract(tail[:, :S], put_real, ((0,), (0,))) + contract(tail[:, S:], put_imag, ((0,), (0,)))
    corner_row = lax.broadcasted_iota(jnp.int32, (ROWS, S), 0)
    corner_lane = lax.broadcasted_iota(jnp.int32, (ROWS, S), 1)
    corner = jnp.where(
        corner_row > 0, 0.0,
        jnp.where(
            corner_lane == 0, dirty[S + 2:S + 3, 0:1],
            jnp.where(corner_lane == 1, dirty[S + 2:S + 3, S:S + 1], 0.0),
        ),
    )
    grid += (0.5 * LOOP_GAIN * WEIGHT) * lanes(dirty, stack(ends, corner))
    _, folded_model = slot_model(grid.astype(BF16))
    ext_row = lax.broadcasted_iota(jnp.int32, (EXT, 2 * S), 0)
    share = jnp.where(
        ext_row == 0, jnp.where(row_block == 0, 0.5, 1.0),
        jnp.where(ext_row < S, 1.0, jnp.where((ext_row == S) & (row_block == 1), 0.5, 0.0)),
    )
    model = fold_buf[...] - folded_model
    column_transform(lanes(dirty * share + model[:, :2 * S], model[:, 2 * S:]))
    out_ref[...] = image_rows() * WEIGHT

    wait_for(column_buf.at[0, pl.ds(0, DEVICES - 1)], send_sems.at[0])
    wait_for(column_buf.at[1, pl.ds(0, DEVICES - 1), :, pl.ds(0, 2 * S)], send_sems.at[2])
    wait_for(u_buf.at[pl.ds(0, P_SIZE - ROWS), :], send_sems.at[1])
    for f in range(F):
        wait_for(first_in.at[f], dirty_send.at[0, f])
    wait_for(second_in.at[pl.ds(0, 7)], dirty_send.at[1, 0])


def imaging(*operands):
    hbm = pl.BlockSpec(memory_space=pltpu.HBM)
    return pl.pallas_call(
        imaging_kernel,
        out_shape=jax.ShapeDtypeStruct((F * ROWS, P_SIZE), F32),
        in_specs=[hbm] * 9,
        out_specs=pl.BlockSpec(memory_space=pltpu.VMEM),
        scratch_shapes=[
            pltpu.SMEM((TILE_CAP,), jnp.int32),
            pltpu.SMEM((TILE_CAP,), jnp.int32),
            pltpu.SMEM((TILE_CAP,), jnp.int32),
            pltpu.SMEM((1,), jnp.int32),
            pltpu.VMEM((2, F * ROWS, P_SIZE), BF16),
            pltpu.VMEM((2, P_SIZE, P_SIZE), BF16),
            pltpu.VMEM((P_SIZE, P_SIZE), BF16),
            pltpu.VMEM((WPLANES, 2, S, S), BF16),
            pltpu.VMEM((TILE_CAP, 2, S, S), BF16),
            pltpu.VMEM((WPLANES, S, 2 * S), BF16),
            pltpu.VMEM((WPLANES, 2 * S, 2 * S), BF16),
            pltpu.VMEM((TILE_CAP + 1, S, 2 * S), F32),
            pltpu.VMEM((NP, S, 2 * S), BF16),
            pltpu.VMEM((2 * P_SIZE + S, P_SIZE), BF16),
            pltpu.VMEM((P_SIZE, 2 * P_SIZE), BF16),
            pltpu.VMEM((2, F * ROWS, 4 * WIDE), BF16),
            pltpu.VMEM((2, DEVICES, ROWS, WIDE), BF16),
            pltpu.VMEM((P_SIZE, WIDE), BF16),
            pltpu.VMEM((8, F * ROWS, WIDE), BF16),
            pltpu.VMEM((F * ROWS, P_SIZE), F32),
            pltpu.VMEM((WPLANES * S, 2 * S), BF16),
            pltpu.VMEM((WPLANES * 2 * S, 2 * S), BF16),
            pltpu.VMEM((2 * S, WPLANES * 2 * S), BF16),
            pltpu.VMEM((2 * S, WIDE), BF16),
            pltpu.VMEM((F, 2, 4, EXT, 2 * S), BF16),
            pltpu.VMEM((F, 3, 2, EXT, 2 * S), BF16),
            pltpu.VMEM((F, 2, EXT, 2 * S), BF16),
            pltpu.VMEM((8, EXT, 2 * S), BF16),
            pltpu.VMEM((EXT, WIDE), F32),
            pltpu.SMEM((SLOTS,), jnp.int32),
            pltpu.SemaphoreType.DMA((8,)),
            pltpu.SemaphoreType.DMA((CHUNKS,)),
            pltpu.SemaphoreType.DMA((3,)),
            pltpu.SemaphoreType.DMA((3,)),
            pltpu.SemaphoreType.DMA((2, F)),
            pltpu.SemaphoreType.DMA((2, F)),
        ],
        compiler_params=pltpu.CompilerParams(
            collective_id=0, has_side_effects=True, vmem_limit_bytes=56 << 20
        ),
        name="imaging",
    )(*operands)


def dft_tables():
    phases = np.outer(np.arange(P_SIZE), np.arange(P_SIZE)) % P_SIZE
    angles = phases * (2.0 * math.pi / P_SIZE)
    tables = np.stack([np.cos(angles), np.sin(angles)]) / math.sqrt(P_SIZE)
    edges = np.zeros((P_SIZE, 4, S))
    for c in range(4):
        edges[:, c, 0] = tables[0, :, (c + 1) % 4 * S]
        edges[:, c, 1] = -tables[1, :, (c + 1) % 4 * S]
    return tables.astype(BF16), edges.reshape(P_SIZE, P_SIZE).astype(BF16)


def local(model_input, w_kernels, visibilities, tile_facet, tile_patch, tile_wplane, tile_count):
    sky = model_input.reshape(2, F * ROWS, P_SIZE)
    cosines, edges = dft_tables()
    image = imaging(
        tile_facet, tile_patch, tile_wplane, tile_count,
        sky, jnp.asarray(cosines), jnp.asarray(edges), w_kernels, visibilities,
    )
    return image.reshape(F, ROWS, P_SIZE)


def solution(mesh):
    return jax.shard_map(
        local,
        mesh=mesh,
        in_specs=(
            P(None, "freq", "vis", None),
            P("freq", None, None, None),
            P(("freq", "vis"), None, None, None),
            P(("freq", "vis")),
            P(("freq", "vis")),
            P(("freq", "vis")),
            P(("freq", "vis")),
        ),
        out_specs=P("freq", "vis", None),
        check_vma=False,
    )
```
